32 devices in a mesh: dp: 8 (over z, core), mp: 4 (over y, x).
Axes of the slice: x: 2, y: 2, z: 4, core: 2. Of those that a mesh axis runs over, the one named last changes fastest.
Arguments:
- activations: bfloat16 [4096, 8192], P('dp', 'mp')
- value_grad: bfloat16 [4096, 1024], P('dp'), may hold values from -6 to 6
- master: float32 [8192, 1024], P(('mp', 'dp')), may hold values from -6 to 6
- first_moment: float32 [8192, 1024], P(('mp', 'dp')), may hold values from -2 to 2
- second_moment: float32 [8192, 1024], P(('mp', 'dp')), may hold values from 0.05 to 1
- step_count: int32 [1], replicated, may hold values from 1 to 40
Outputs:
- new_master: float32 [8192, 1024], P(('mp', 'dp'))
- new_first: float32 [8192, 1024], P(('mp', 'dp'))
- new_second: float32 [8192, 1024], P(('mp', 'dp'))
- rollout_update: bfloat16 [8192, 1024], P(None, 'mp')
The draws below stay inside these ranges and needn't reach their ends.
Inputs may be any that keep to these rules, and one draw needn't show every extreme that they name: `step_count`: the number of optimizer steps taken so far, this one included.
All inputs are finite; a program needn't handle non-finite values.
Results may differ from the reference program's by a relative error of at most 0.0004.
Values may be sent and summed in bfloat16 or wider, within the bound.
A program may use at most 64 MiB of HBM per device.

```python
import math
import jax
import jax.numpy as jnp
from jax import lax

D = 8192
KV = 1024
TOKENS = 4096


def draw_activations(key, part):
    key_base, key_spread = jax.random.split(key, 2)
    values_drawn = jax.random.normal(key_base, (TOKENS, D), jnp.float32)
    column_ramp = jnp.exp(jnp.log(3.0) * jnp.arange(D, dtype=jnp.float32) / D)
    column_spread = 10.0 ** jax.random.uniform(key_spread, (D,), jnp.float32) / 3.0
    values_drawn = jnp.clip(values_drawn * column_ramp * column_spread, -40.0, 40.0)
    return values_drawn.astype(jnp.bfloat16)


def block_scale(stream_key, dims, pieces, smallest, high):
    level, own = 1.0, jax.random.fold_in(stream_key, 6)
    for axis_at, blocks in pieces:
        draws = jnp.exp(jax.random.uniform(jax.random.fold_in(own, axis_at), (blocks,), jnp.float32, smallest / len(pieces), high / len(pieces)))
        level = level * jnp.repeat(draws, dims[axis_at] // blocks).reshape([-1 if axis == axis_at else 1 for axis in range(len(dims))])
    return level


def normal_values(stream_key, dims, width, most, pieces=(), kind=jnp.bfloat16):
    result = width * jax.random.normal(stream_key, dims, jnp.float32)
    if pieces:
        result = result * block_scale(stream_key, dims, pieces, -0.22, 0.18)
    return jnp.clip(result, -most, most).astype(kind)


def setup_inputs(seed: int = 0) -> dict:
    arg_keys = jax.random.split(jax.random.key(seed), 7)
    activations = draw_activations(jax.random.fold_in(arg_keys[6], 71), 0)
    value_grad = normal_values(arg_keys[1], (TOKENS, KV), 1.0, 6.0, ((0, 8),))
    master = normal_values(arg_keys[2], (D, KV), 1.0, 6.0, ((0, 32),), jnp.float32)
    first_moment = normal_values(arg_keys[3], (D, KV), 0.3, 2.0, ((0, 32),), jnp.float32)
    second_moment = jnp.clip(jnp.exp(math.log(1.0) - 2.9957323 * jax.random.uniform(arg_keys[4], (D, KV), jnp.float32) ** block_scale(arg_keys[4], (D, KV), ((0, 32),), -0.2, 0.2)), 0.05, 1.0)
    step_count = jax.random.randint(arg_keys[5], (1,), 1, 41).astype(jnp.int32)
    return {"activations": activations, "value_grad": value_grad, "master": master, "first_moment": first_moment, "second_moment": second_moment, "step_count": step_count}


def reference(activations, value_grad, master, first_moment, second_moment, step_count):
    grad = lax.dot_general(activations, value_grad, (((0,), (0,)), ((), ())), preferred_element_type=jnp.float32)
    norm_value = jnp.sqrt(jnp.sum(grad * grad))
    clip_total = 0.5 * jnp.sqrt(jnp.float32(D * KV))
    factor = jnp.minimum(jnp.float32(1.0), clip_total / (norm_value + 1e-06))
    clipped = factor * grad
    new_first = 0.9 * first_moment + 0.1 * clipped
    new_second = 0.95 * second_moment + 0.05 * clipped * clipped
    steps_done = step_count[0].astype(jnp.float32)
    bias_first = 1.0 - jnp.exp(steps_done * jnp.log(jnp.float32(0.9)))
    bias_second = 1.0 - jnp.exp(steps_done * jnp.log(jnp.float32(0.95)))
    direction = new_first / bias_first / (jnp.sqrt(new_second / bias_second) + 1e-08) + 0.1 * master
    new_master = master - 0.01 * direction
    return (new_master, new_first, new_second, direction.astype(jnp.bfloat16))
```

```python
import functools
import math

import jax
import jax.numpy as jnp
from jax import lax
from jax.experimental import pallas as pl
from jax.experimental.pallas import tpu as pltpu
from jax.sharding import PartitionSpec as P

F32 = jnp.float32
LEVELS = 32760.0
PIECES = (1, 1, 1, 4)
RES = 2
LAG = 2
MESH = pl.DeviceIdType.MESH


def adam_terms(step):
    bias_first = 1.0 - jnp.exp(step * jnp.float32(math.log(0.9)))
    bias_second = 1.0 - jnp.exp(step * jnp.float32(math.log(0.95)))
    return 1.0 / bias_first, 1.0 / bias_second


def kernel(
    line,
    heads,
    clip_total,
    step_ref,
    act_ref,
    vg_ref,
    master_ref,
    first_ref,
    second_ref,
    new_master_ref,
    new_first_ref,
    new_second_ref,
    rollout_ref,
    act,
    vg,
    acc,
    q_out,
    s_out,
    q_in,
    s_in,
    squares,
    norms,
    w_in,
    m_in,
    v_in,
    w_out,
    m_out,
    v_out,
    update,
    in_sem,
    pair_send,
    pair_recv,
    load_sem,
    rs_send,
    rs_recv,
    meet,
    norm_send,
    norm_recv,
    store_sem,
    a2a_send,
    a2a_recv,
    up_send,
    down_send,
    chain_recv,
    mate_send,
    mate_recv,
):
    dpn = 2 * line
    dp = lax.axis_index("dp")
    mp = lax.axis_index("mp")
    z = dp // 2
    core = lax.rem(dp, 2)
    mate = dp + 1 - 2 * core
    tokens = act_ref.shape[0]
    rows = master_ref.shape[0]
    cols = master_ref.shape[1]
    head_cols = cols // heads
    tile = head_cols // 2
    chunks = 2 * heads
    half = rows // 2

    lower = z < line // 2
    at_end = (z == 0) | (z == line - 1)
    end = jnp.where(lower, 0, line - 1)
    mid = jnp.where(lower, 1, line - 2)
    far_mid = line - 1 - mid
    far_end = line - 1 - end
    toward = jnp.where(lower, 2, -2)
    ahead = dp + toward
    behind = jnp.where(at_end, dp, dp - toward)

    def peer(slot):
        return lax.rem(mp // 2 + slot // 2, heads // 2) * 2 + lax.rem(mp + slot % 2, 2)

    def source(slot):
        y = lax.rem(mp // 2 + heads // 2 - slot // 2, heads // 2)
        return y * 2 + lax.rem(mp + slot % 2, 2)

    barrier = pltpu.get_barrier_semaphore()
    pl.semaphore_signal(barrier, inc=1, device_id={"dp": mate}, device_id_type=MESH)
    pl.semaphore_signal(barrier, inc=1, device_id={"dp": ahead}, device_id_type=MESH)

    @pl.when(jnp.logical_not(at_end))
    def _():
        pl.semaphore_signal(barrier, inc=1, device_id={"dp": behind}, device_id_type=MESH)

    for slot in (1, 2):
        pl.semaphore_signal(barrier, inc=1, device_id={"mp": peer(slot)}, device_id_type=MESH)

    def own_act(dest):
        start = pl.multiple_of((dest * 2 + core) * rows, rows)
        return pltpu.make_async_copy(
            act_ref.at[:, pl.ds(start, rows)],
            act.at[dest, pl.ds(0, tokens)],
            in_sem.at[dest],
        )

    def head_lanes(slot):
        return pl.ds(pl.multiple_of(peer(slot) * head_cols, head_cols), head_cols)

    def chunk_lanes(k):
        at = peer(k // 2) * 2 + k % 2
        return pl.ds(pl.multiple_of(at * tile, tile), tile)

    def own_vg(slot):
        at = head_lanes(slot)
        return pltpu.make_async_copy(
            vg_ref.at[:, at], vg.at[pl.ds(0, tokens), at], in_sem.at[line + slot]
        )

    def pair_act(dest):
        start = pl.multiple_of((dest * 2 + 1 - core) * rows, rows)
        return pltpu.make_async_remote_copy(
            src_ref=act_ref.at[:, pl.ds(start, rows)],
            dst_ref=act.at[dest, pl.ds(tokens, tokens)],
            send_sem=pair_send.at[dest],
            recv_sem=pair_recv.at[dest],
            device_id={"dp": mate},
            device_id_type=MESH,
        )

    def pair_vg(slot):
        at = head_lanes(slot)
        return pltpu.make_async_remote_copy(
            src_ref=vg_ref.at[:, at],
            dst_ref=vg.at[pl.ds(tokens, tokens), at],
            send_sem=pair_send.at[line + slot],
            recv_sem=pair_recv.at[line + slot],
            device_id={"dp": mate},
            device_id_type=MESH,
        )

    order = [
        far_end,
        jnp.where(at_end, far_mid, end),
        jnp.where(at_end, mid, far_mid),
        jnp.where(at_end, end, mid),
    ]
    own_act(order[0]).start()
    for slot in range(heads):
        own_vg(slot).start()
    for dest in order[1:]:
        own_act(dest).start()
    loads = [
        pltpu.make_async_copy(src, dst, load_sem.at[i])
        for i, (src, dst) in enumerate(
            ((master_ref, w_in), (first_ref, m_in), (second_ref, v_in))
        )
    ]
    with jax.named_scope("bar"):
        pl.semaphore_wait(barrier, jnp.where(at_end, 4, 5))
    pair_act(order[0]).start()
    for slot in range(heads):
        pair_vg(slot).start()
    for dest in order[1:]:
        pair_act(dest).start()
    for copy in loads:
        copy.start()

    def ready(dest):
        own_act(dest).wait()
        pair_act(dest).wait_recv()

    def multiply(dest, slot):
        at = head_lanes(slot)
        acc[dest, :, at] = lax.dot_general(
            act[dest], vg[:, at], (((0,), (0,)), ((), ())), preferred_element_type=F32
        )

    def hop(dest, k, way, to):
        data = pltpu.make_async_remote_copy(
            src_ref=q_out.at[dest, k],
            dst_ref=q_in.at[way, dest, k],
            send_sem=rs_send.at[0, dest, k],
            recv_sem=rs_recv.at[0, way, dest, k],
            device_id={"dp": to},
            device_id_type=MESH,
        )
        scale = pltpu.make_async_remote_copy(
            src_ref=s_out.at[dest, k],
            dst_ref=s_in.at[way, dest, k],
            send_sem=rs_send.at[1, dest, k],
            recv_sem=rs_recv.at[1, way, dest, k],
            device_id={"dp": to},
            device_id_type=MESH,
        )
        return data, scale

    def take(dest, k, way):
        for copy in hop(dest, k, way, ahead):
            copy.wait_recv()
        top = s_in[way, dest, k] * (1.0 / LEVELS)
        got = q_in[way, dest, k].astype(jnp.int32).astype(F32)
        return acc[dest, :, chunk_lanes(k)] + got * top

    def give(total, dest, k, way, to):
        top = jnp.maximum(jnp.max(jnp.abs(total), axis=0, keepdims=True), 1e-30)
        s_out[dest, k] = top
        q_out[dest, k] = jnp.round(total * (LEVELS / top)).astype(jnp.int32).astype(jnp.int16)
        for copy in hop(dest, k, way, to):
            copy.start()

    def add_squares(total):
        squares[...] += jnp.sum((total * total).reshape(rows // 8, 8, tile), axis=0)

    def place(i, first, second):
        dest = jnp.where(i < chunks, first, second)
        return dest, jnp.where(i < chunks, i, lax.rem(i + RES, chunks))

    squares[...] = jnp.zeros(squares.shape, F32)

    with jax.named_scope("w0"):
        ready(order[0])

    def hello(stage):
        slot = stage + 1
        pl.semaphore_signal(
            meet.at[stage], inc=1, device_id={"mp": peer(slot)}, device_id_type=MESH
        )

    def heard(stage):
        pl.semaphore_wait(meet.at[stage], 1)

    @pl.when(at_end)
    def _():
        def send(dest, k):
            give(acc[dest, :, chunk_lanes(k)], dest, k, 0, ahead)

        for slot in range(heads):
            own_vg(slot).wait()
            pair_vg(slot).wait_recv()
            with jax.named_scope(f"Em{slot}"):
                multiply(far_end, slot)
            with jax.named_scope(f"Eg{slot}"):
                send(far_end, 2 * slot)
                send(far_end, 2 * slot + 1)

        with jax.named_scope("Erest"):
            ready(far_mid)

            @pl.loop(0, heads)
            def _(step):
                slot = lax.rem(step + RES // 2, heads)
                multiply(far_mid, slot)
                send(far_mid, 2 * slot)
                send(far_mid, 2 * slot + 1)

            ready(mid)

            @pl.loop(0, heads)
            def _(slot):
                multiply(mid, slot)
                send(mid, 2 * slot)
                send(mid, 2 * slot + 1)

            ready(end)

            @pl.loop(0, heads)
            def _(slot):
                multiply(end, slot)

        @pl.loop(0, 2 * chunks - RES)
        def _(j):
            with jax.named_scope("Et"):
                dest, k = place(j, end, mid)
                total = take(dest, k, 1)
                add_squares(total)

                @pl.when(j < chunks)
                def _():
                    acc[dest, :, chunk_lanes(k)] = total

                @pl.when(j == 1)
                def _():
                    hello(0)

                @pl.when(j == chunks // 2)
                def _():
                    heard(0)
                    hello(1)

        heard(1)

    @pl.when(jnp.logical_not(at_end))
    def _():
        for slot in range(heads):
            own_vg(slot).wait()
            pair_vg(slot).wait_recv()
            multiply(far_end, slot)
        ready(end)

        @pl.loop(0, heads)
        def _(slot):
            multiply(end, slot)

        ready(far_mid)
        ready(mid)

        def onward(j):
            dest, k = place(j, end, mid)
            total = take(dest, k, 1)

            @pl.when(j < 2 * chunks - RES)
            def _():
                give(total, dest, k, 1, behind)

            @pl.when(j >= chunks)
            def _():
                acc[dest, :, chunk_lanes(k)] = total

        @pl.loop(0, 2 * chunks)
        def _(i):
            with jax.named_scope("Mn"):
                dest, k = place(i, far_end, far_mid)
                give(take(dest, k, 0), dest, k, 1, ahead)

            @pl.when(i < chunks)
            def _():
                multiply(jnp.where(i < heads, far_mid, mid), lax.rem(i, heads))

            @pl.when(i >= LAG)
            def _():
                with jax.named_scope("Mf"):
                    onward(i - LAG)

            @pl.when(i == LAG + 1)
            def _():
                hello(0)

            @pl.when(i == LAG + chunks // 2)
            def _():
                heard(0)
                hello(1)

        @pl.loop(2 * chunks - LAG, 2 * chunks - RES)
        def _(j):
            with jax.named_scope("Mf"):
                onward(j)

        for k in range(RES):
            with jax.named_scope("Mr"):
                onward(2 * chunks - RES + k)
                total = take(mid, k, 0)
                acc[mid, :, chunk_lanes(k)] = total
                add_squares(total)

        heard(1)

    me = dp * heads + mp
    norms[me] = jnp.sum(squares[...], axis=0, keepdims=True)

    def norm_to(step, slot):
        at = step * heads + slot
        return pltpu.make_async_remote_copy(
            src_ref=norms.at[me],
            dst_ref=norms.at[me],
            send_sem=norm_send.at[at],
            recv_sem=norm_recv.at[at],
            device_id={"dp": lax.rem(dp + step, dpn), "mp": lax.rem(mp + slot, heads)},
            device_id_type=MESH,
        )

    others = [(step, slot) for step in range(dpn) for slot in range(heads) if step + slot]
    with jax.named_scope("ns"):
        for step, slot in others:
            norm_to(step, slot).start()
    for copy in loads:
        copy.wait()
    with jax.named_scope("nw"):
        for step, slot in others:
            norm_to(step, slot).wait_recv()
    square_sum = jnp.sum(jnp.sum(norms[...], axis=0), keepdims=True)
    factor = jnp.minimum(1.0, clip_total / (jnp.sqrt(square_sum) + 1e-06))
    step_count = jnp.full((1, 1), step_ref[0].astype(F32), F32)
    scale_first, scale_second = adam_terms(step_count)

    def block(owner, origin, part):
        start = (owner * dpn + origin) * rows + part * half
        return rollout_ref.at[pl.ds(pl.multiple_of(start, half), half)]

    def piece(head, part):
        return update.at[head, pl.ds(part * half, half)]

    def mine(part):
        return pltpu.make_async_copy(
            piece(mp, part), block(mp, dp, part), store_sem.at[3 + part]
        )

    def to_head(slot, part):
        return pltpu.make_async_remote_copy(
            src_ref=piece(peer(slot), part),
            dst_ref=block(mp, dp, part),
            send_sem=a2a_send.at[slot, part],
            recv_sem=a2a_recv.at[slot, part],
            device_id={"mp": peer(slot)},
            device_id_type=MESH,
        )

    def relay(ref, owner, at_z, part, send, recv, to):
        return pltpu.make_async_remote_copy(
            src_ref=ref,
            dst_ref=block(owner, at_z * 2 + core, part),
            send_sem=send.at[at_z, owner, part],
            recv_sem=recv.at[at_z, owner, part],
            device_id={"dp": to},
            device_id_type=MESH,
        )

    def send_up(ref, owner, at_z, part):
        return relay(ref, owner, at_z, part, up_send, chain_recv, dp + 2)

    def send_down(ref, owner, at_z, part):
        return relay(ref, owner, at_z, part, down_send, chain_recv, dp - 2)

    def send_mate(ref, owner, at_z, part):
        return relay(ref, owner, at_z, part, mate_send, mate_recv, mate)

    def spread(ref, owner, part):
        @pl.when(z < line - 1)
        def _():
            send_up(ref, owner, z, part).start()

        @pl.when(z > 0)
        def _():
            send_down(ref, owner, z, part).start()

        send_mate(ref, owner, z, part).start()

    slab = min(32, half)

    def step_rows(slot, part):
        lanes = head_lanes(slot)

        @pl.loop(0, half // slab)
        def _(r):
            at = pl.ds(pl.multiple_of(part * half + r * slab, slab), slab)
            clipped = acc[z, at, lanes] * factor
            weight = w_in[at, lanes]
            first = 0.9 * m_in[at, lanes] + 0.1 * clipped
            second = 0.95 * v_in[at, lanes] + 0.05 * clipped * clipped
            m_out[at, lanes] = first
            v_out[at, lanes] = second
            direction = (first * scale_first) / (
                jnp.sqrt(second * scale_second) + 1e-08
            ) + 0.1 * weight
            w_out[at, lanes] = weight - 0.01 * direction
            update[peer(slot), at, :] = direction.astype(jnp.bfloat16)

    def late(slot):
        @pl.when(jnp.logical_not(at_end))
        def _():
            for k in (2 * slot, 2 * slot + 1):
                acc[mid, :, chunk_lanes(k)] = take(mid, k, 0)

    work = [(0, 0), (1, 0), (2, 0), (0, 1), (1, 1), (2, 1), (3, 0), (3, 1)]
    for slot, part in work:
        with jax.named_scope(f"up{slot}{part}"):
            if part == 0 and 2 * slot >= RES:
                late(slot)
            step_rows(slot, part)
            if slot == 0:
                mine(part).start()
                spread(piece(mp, part), mp, part)
            else:
                to_head(slot, part).start()

    stores = [
        pltpu.make_async_copy(src, dst, store_sem.at[i])
        for i, (src, dst) in enumerate(
            ((w_out, new_master_ref), (m_out, new_first_ref), (v_out, new_second_ref))
        )
    ]
    for copy in stores:
        copy.start()

    for slot, part in work:
        if slot:
            with jax.named_scope(f"aa{slot}{part}"):
                to_head(slot, part).wait_recv()
                spread(block(source(slot), dp, part), source(slot), part)

    arrivals = [(0, 0), (0, 1)] + [w for w in work if w[0]]
    for far in range(1, line):
        with jax.named_scope(f"far{far}"):
            for slot, part in arrivals:
                owner = source(slot)

                @pl.when(z - far >= 0)
                def _():
                    at_z = z - far
                    ref = block(owner, at_z * 2 + core, part)
                    send_up(ref, owner, at_z, part).wait_recv()

                    @pl.when(z < line - 1)
                    def _():
                        send_up(ref, owner, at_z, part).start()

                    send_mate(ref, owner, at_z, part).start()

                @pl.when(z + far < line)
                def _():
                    at_z = z + far
                    ref = block(owner, at_z * 2 + core, part)
                    send_down(ref, owner, at_z, part).wait_recv()

                    @pl.when(z > 0)
                    def _():
                        send_down(ref, owner, at_z, part).start()

                    send_mate(ref, owner, at_z, part).start()

    with jax.named_scope("tail"):
        for at_z in range(line):
            for owner in range(heads):
                for part in range(2):
                    ref = block(owner, at_z * 2 + core, part)
                    send_mate(ref, owner, at_z, part).wait_recv()
                    send_mate(ref, owner, at_z, part).wait_send()

                    @pl.when((z < line - 1) & (z >= at_z))
                    def _():
                        send_up(ref, owner, at_z, part).wait_send()

                    @pl.when((z > 0) & (z <= at_z))
                    def _():
                        send_down(ref, owner, at_z, part).wait_send()

        for slot in range(1, heads):
            for part in range(2):
                to_head(slot, part).wait_send()
        for step, slot in others:
            norm_to(step, slot).wait_send()
        for dest in range(line):
            pair_act(dest).wait_send()
        for slot in range(heads):
            pair_vg(slot).wait_send()

        def sent(dest, k):
            for copy in hop(dest, k, 0, ahead):
                copy.wait_send()

        @pl.loop(0, chunks)
        def _(k):
            sent(far_end, k)
            sent(far_mid, k)
            sent(jnp.where(at_end, mid, end), k)

            @pl.when(jnp.logical_not(at_end) & (k >= RES))
            def _():
                sent(mid, k)

        for part in range(2):
            mine(part).wait()
        for copy in stores:
            copy.wait()


def settle(*refs):
    count = (len(refs) - 1) // 2
    sem = refs[-1]
    copies = []
    for i in range(count):
        source, place = refs[i], refs[count + i]
        piece = source.shape[0] // PIECES[i]
        for j in range(PIECES[i]):
            at = pl.ds(j * piece, piece)
            copies.append(
                pltpu.make_async_copy(source.at[at], place.at[at], sem.at[len(copies)])
            )
    for copy in copies:
        copy.start()
    for copy in copies:
        copy.wait()


def one_kernel(line, heads, activations, value_grad, master, first_moment, second_moment, step_count):
    rows, cols = master.shape
    tokens = activations.shape[0]
    tile = cols // heads // 2
    chunks = 2 * heads
    dpn = 2 * line
    clip_total = 0.5 * math.sqrt(rows * dpn * heads * cols)
    hbm = pl.BlockSpec(memory_space=pl.ANY)
    owned = jax.ShapeDtypeStruct((rows, cols), F32)
    wide = pltpu.VMEM((rows, cols), F32)
    dma = pltpu.SemaphoreType.DMA
    results = pl.pallas_call(
        functools.partial(kernel, line, heads, clip_total),
        out_shape=(
            owned,
            owned,
            owned,
            jax.ShapeDtypeStruct((rows * dpn * heads, cols // heads), jnp.bfloat16),
        ),
        in_specs=[pl.BlockSpec(memory_space=pltpu.SMEM)]
        + [hbm] * 5,
        out_specs=(hbm,) * 4,
        scratch_shapes=[
            pltpu.VMEM((line, 2 * tokens, rows), jnp.bfloat16),
            pltpu.VMEM((2 * tokens, cols), jnp.bfloat16),
            pltpu.VMEM((line, rows, cols), F32),
            pltpu.VMEM((line, chunks, rows, tile), jnp.int16),
            pltpu.VMEM((line, chunks, 1, tile), F32),
            pltpu.VMEM((2, line, chunks, rows, tile), jnp.int16),
            pltpu.VMEM((2, line, chunks, 1, tile), F32),
            pltpu.VMEM((8, tile), F32),
            pltpu.VMEM((dpn * heads, 1, tile), F32),
            wide,
            wide,
            wide,
            wide,
            wide,
            wide,
            pltpu.VMEM((heads, rows, cols // heads), jnp.bfloat16),
            dma((line + heads,)),
            dma((line + heads,)),
            dma((line + heads,)),
            dma((3,)),
            dma((2, line, chunks)),
            dma((2, 2, line, chunks)),
            pltpu.SemaphoreType.REGULAR((2,)),
            dma((dpn * heads,)),
            dma((dpn * heads,)),
            dma((5,)),
            dma((heads, 2)),
            dma((heads, 2)),
            dma((line, heads, 2)),
            dma((line, heads, 2)),
            dma((line, heads, 2)),
            dma((line, heads, 2)),
            dma((line, heads, 2)),
        ],
        compiler_params=pltpu.CompilerParams(
            collective_id=0, has_side_effects=True, vmem_limit_bytes=28 * 1024 * 1024
        ),
    )(
        step_count,
        *(
            pltpu.with_memory_space_constraint(x, pltpu.HBM)
            for x in (activations, value_grad, master, first_moment, second_moment)
        ),
    )
    shapes = tuple(jax.ShapeDtypeStruct(x.shape, x.dtype) for x in results)
    return pl.pallas_call(
        settle,
        out_shape=shapes,
        in_specs=[hbm] * 4,
        out_specs=(hbm,) * 4,
        scratch_shapes=[dma((sum(PIECES),))],
        compiler_params=pltpu.CompilerParams(vmem_limit_bytes=4 * 1024 * 1024),
    )(*(pltpu.with_memory_space_constraint(x, pltpu.VMEM) for x in results))


def plain(activations, value_grad, master, first_moment, second_moment, step_count):
    own_rows, cols = master.shape
    grad = lax.psum_scatter(
        lax.dot_general(
            activations, value_grad, (((0,), (0,)), ((), ())), preferred_element_type=F32
        ),
        "dp",
        scatter_dimension=0,
        tiled=True,
    )
    square_sum = lax.psum(jnp.sum(grad * grad), ("dp", "mp"))
    head_count = lax.axis_size("mp")
    clip_total = 0.5 * math.sqrt(own_rows * lax.axis_size("dp") * head_count * cols)
    factor = jnp.minimum(jnp.float32(1.0), clip_total / (jnp.sqrt(square_sum) + 1e-06))
    clipped = factor * grad
    new_first = 0.9 * first_moment + 0.1 * clipped
    new_second = 0.95 * second_moment + 0.05 * clipped * clipped
    scale_first, scale_second = adam_terms(step_count[0].astype(F32))
    direction = new_first * scale_first / (jnp.sqrt(new_second * scale_second) + 1e-08) + 0.1 * master
    new_master = master - 0.01 * direction
    update = direction.astype(jnp.bfloat16)
    received = lax.all_to_all(update, "mp", split_axis=1, concat_axis=0, tiled=True)
    stacked = received.reshape(head_count, own_rows, received.shape[1])
    gathered = lax.all_gather(stacked, "dp", axis=1, tiled=True)
    return (new_master, new_first, new_second, gathered.reshape(-1, gathered.shape[2]))


def solution(mesh):
    dpn, heads = mesh.shape["dp"], mesh.shape["mp"]

    def on_device(*args):
        rows, cols = args[2].shape
        if dpn == 8 and heads == 4 and rows % 64 == 0 and (cols // heads) % 256 == 0:
            return one_kernel(dpn // 2, heads, *args)
        return plain(*args)

    in_specs = (
        P("dp", "mp"),
        P("dp", None),
        P(("mp", "dp"), None),
        P(("mp", "dp"), None),
        P(("mp", "dp"), None),
        P(),
    )
    out_specs = (P(("mp", "dp"), None), P(("mp", "dp"), None), P(("mp", "dp"), None), P(None, "mp"))
    return jax.shard_map(
        on_device, mesh=mesh, in_specs=in_specs, out_specs=out_specs, check_vma=False
    )
```

```python
import functools
import math

import jax
import jax.numpy as jnp
from jax import lax
from jax.experimental import pallas as pl
from jax.experimental.pallas import tpu as pltpu
from jax.sharding import PartitionSpec as P

F32 = jnp.float32
LEVELS = 32760.0
PIECES = (1, 1, 1, 4)
RES = 4
LAG = 4
EARLY = 4
MESH = pl.DeviceIdType.MESH


def adam_terms(step):
    bias_first = 1.0 - jnp.exp(step * jnp.float32(math.log(0.9)))
    bias_second = 1.0 - jnp.exp(step * jnp.float32(math.log(0.95)))
    return 1.0 / bias_first, 1.0 / bias_second


def kernel(
    line,
    heads,
    clip_total,
    step_ref,
    act_ref,
    vg_ref,
    master_ref,
    first_ref,
    second_ref,
    new_master_ref,
    new_first_ref,
    new_second_ref,
    rollout_ref,
    act,
    vg,
    acc,
    q_out,
    s_out,
    q_in,
    s_in,
    squares,
    norms,
    tally,
    w_in,
    m_in,
    v_in,
    w_out,
    m_out,
    v_out,
    update,
    in_sem,
    pair_send,
    pair_recv,
    load_sem,
    rs_send,
    near_recv,
    wide_recv,
    meet,
    norm_sem,
    store_sem,
    a2a_send,
    a2a_recv,
    spread_send,
    chain_recv,
    mate_recv,
):
    dpn = 2 * line
    dp = lax.axis_index("dp")
    mp = lax.axis_index("mp")
    z = dp // 2
    core = lax.rem(dp, 2)
    mate = dp + 1 - 2 * core
    tokens = act_ref.shape[0]
    rows = master_ref.shape[0]
    cols = master_ref.shape[1]
    head_cols = cols // heads
    tile = head_cols // 2
    half = rows // 2
    units = 4 * heads

    lower = z < line // 2
    at_end = (z == 0) | (z == line - 1)
    end = jnp.where(lower, 0, line - 1)
    mid = jnp.where(lower, 1, line - 2)
    far_mid = line - 1 - mid
    far_end = line - 1 - end
    toward = jnp.where(lower, 2, -2)
    ahead = dp + toward
    behind = jnp.where(at_end, dp, dp - toward)

    def peer(slot):
        return lax.rem(mp // 2 + slot // 2, heads // 2) * 2 + lax.rem(mp + slot % 2, 2)

    def source(slot):
        y = lax.rem(mp // 2 + heads // 2 - slot // 2, heads // 2)
        return y * 2 + lax.rem(mp + slot % 2, 2)

    barrier = pltpu.get_barrier_semaphore()
    pl.semaphore_signal(barrier, inc=1, device_id={"dp": mate}, device_id_type=MESH)
    pl.semaphore_signal(barrier, inc=1, device_id={"dp": ahead}, device_id_type=MESH)

    @pl.when(jnp.logical_not(at_end))
    def _():
        pl.semaphore_signal(barrier, inc=1, device_id={"dp": behind}, device_id_type=MESH)

    for slot in (1, 2):
        pl.semaphore_signal(barrier, inc=1, device_id={"mp": peer(slot)}, device_id_type=MESH)

    def own_act(dest):
        start = pl.multiple_of((dest * 2 + core) * rows, rows)
        return pltpu.make_async_copy(
            act_ref.at[:, pl.ds(start, rows)],
            act.at[dest, pl.ds(0, tokens)],
            in_sem.at[dest],
        )

    def head_lanes(slot):
        return pl.ds(pl.multiple_of(peer(slot) * head_cols, head_cols), head_cols)

    def chunk_lanes(k):
        at = peer(k // 2) * 2 + k % 2
        return pl.ds(pl.multiple_of(at * tile, tile), tile)

    def unit(k):
        return pl.ds(pl.multiple_of(k % 2 * half, half), half), chunk_lanes(k // 2)

    def own_vg(slot):
        at = head_lanes(slot)
        return pltpu.make_async_copy(
            vg_ref.at[:, at], vg.at[pl.ds(0, tokens), at], in_sem.at[line + slot]
        )

    def pair_act(dest, part=None):
        at = part or 0
        count = rows if part is None else half
        start = pl.multiple_of((dest * 2 + 1 - core) * rows + at * half, half)
        return pltpu.make_async_remote_copy(
            src_ref=act_ref.at[:, pl.ds(start, count)],
            dst_ref=act.at[dest, pl.ds(tokens, tokens), pl.ds(at * half, count)],
            send_sem=pair_send.at[0],
            recv_sem=pair_recv.at[line if part else dest],
            device_id={"dp": mate},
            device_id_type=MESH,
        )

    def pair_vg(slot, part=None):
        at = head_lanes(slot) if part is None else chunk_lanes(2 * slot + part)
        return pltpu.make_async_remote_copy(
            src_ref=vg_ref.at[:, at],
            dst_ref=vg.at[pl.ds(tokens, tokens), at],
            send_sem=pair_send.at[1],
            recv_sem=pair_recv.at[line + 1 + (heads if part else slot)],
            device_id={"dp": mate},
            device_id_type=MESH,
        )

    order = [
        far_end,
        jnp.where(at_end, far_mid, end),
        jnp.where(at_end, mid, far_mid),
        jnp.where(at_end, end, mid),
    ]
    own_act(order[0]).start()
    for slot in range(heads):
        own_vg(slot).start()
    for dest in order[1:]:
        own_act(dest).start()
    loads = [
        pltpu.make_async_copy(src, dst, load_sem.at[i])
        for i, (src, dst) in enumerate(
            ((master_ref, w_in), (first_ref, m_in), (second_ref, v_in))
        )
    ]
    with jax.named_scope("bar"):
        pl.semaphore_wait(barrier, jnp.where(at_end, 4, 5))
    for part in range(2):
        pair_act(order[0], part).start()
        pair_vg(0, part).start()
    for slot in range(1, heads):
        pair_vg(slot).start()
    for dest in order[1:]:
        pair_act(dest).start()
    for copy in loads:
        copy.start()

    def ready(dest):
        own_act(dest).wait()
        pair_act(dest).wait_recv()

    def ready_vg(slot):
        own_vg(slot).wait()
        pair_vg(slot).wait_recv()

    def multiply_unit(dest, part, k):
        at = chunk_lanes(k)
        here = slice(part * half, (part + 1) * half)
        acc[dest, here, at] = lax.dot_general(
            act[dest, :, here], vg[:, at], (((0,), (0,)), ((), ())), preferred_element_type=F32
        )

    def multiply(dest, slot):
        at = head_lanes(slot)
        acc[dest, :, at] = lax.dot_general(
            act[dest], vg[:, at], (((0,), (0,)), ((), ())), preferred_element_type=F32
        )

    def hop(dest, k, way, i, to):
        recv = (near_recv, wide_recv)[way]
        data = pltpu.make_async_remote_copy(
            src_ref=q_out.at[dest, k],
            dst_ref=q_in.at[way, dest, k],
            send_sem=rs_send.at[0, dest],
            recv_sem=recv.at[i],
            device_id={"dp": to},
            device_id_type=MESH,
        )
        scale = pltpu.make_async_remote_copy(
            src_ref=s_out.at[dest, k],
            dst_ref=s_in.at[way, dest, k],
            send_sem=rs_send.at[1, dest],
            recv_sem=recv.at[i],
            device_id={"dp": to},
            device_id_type=MESH,
        )
        return data, scale

    def take(dest, k, way, i):
        pltpu.make_async_copy(tally, tally, (near_recv, wide_recv)[way].at[i]).wait()
        top = s_in[way, dest, k] * (1.0 / LEVELS)
        got = q_in[way, dest, k].astype(jnp.int32).astype(F32)
        return acc[dest, *unit(k)] + got * top

    def give(total, dest, k, way, i, to):
        top = jnp.maximum(jnp.max(jnp.abs(total), axis=0, keepdims=True), 1e-30)
        s_out[dest, k] = top
        q_out[dest, k] = jnp.round(total * (LEVELS / top)).astype(jnp.int32).astype(jnp.int16)
        for copy in hop(dest, k, way, i, to):
            copy.start()

    def add_squares(total):
        squares[...] += jnp.sum((total * total).reshape(half // 8, 8, tile), axis=0)

    def place(i, first, second):
        dest = jnp.where(i < units, first, second)
        return dest, jnp.where(i < units, i, lax.rem(i + RES, units))

    squares[...] = jnp.zeros(squares.shape, F32)

    def hello(stage):
        slot = stage + 1
        pl.semaphore_signal(
            meet.at[stage], inc=1, device_id={"mp": peer(slot)}, device_id_type=MESH
        )

    def heard(stage):
        pl.semaphore_wait(meet.at[stage], 1)

    def send(i):
        dest, k = place(i, far_end, far_mid)
        dest = jnp.where(i < 2 * units, dest, mid)
        k = jnp.where(i < 2 * units, k, i - 2 * units)
        give(acc[dest, *unit(k)], dest, k, 0, i, ahead)

    @pl.when(at_end)
    def _():
        own_act(far_end).wait()
        own_vg(0).wait()
        for k in range(2):
            for part in range(2):
                with jax.named_scope(f"Ew{k}{part}"):
                    if k == 0:
                        pair_act(far_end, part).wait_recv()
                    if part == 0:
                        pair_vg(0, k).wait_recv()
                with jax.named_scope(f"Em{k}{part}"):
                    multiply_unit(far_end, part, k)
                    send(2 * k + part)

        for slot in range(1, heads):
            with jax.named_scope(f"Em{slot}"):
                ready_vg(slot)
                multiply(far_end, slot)
                for k in range(4):
                    send(4 * slot + k)

        with jax.named_scope("Erest"):
            ready(far_mid)

            @pl.loop(0, heads)
            def _(step):
                multiply(far_mid, lax.rem(step + RES // 4, heads))
                for k in range(4):
                    send(units + 4 * step + k)

            ready(mid)

            @pl.loop(0, heads)
            def _(slot):
                multiply(mid, slot)

            @pl.loop(2 * units, 2 * units + RES + EARLY)
            def _(i):
                send(i)

            ready(end)

            @pl.loop(0, heads)
            def _(slot):
                multiply(end, slot)

        @pl.loop(0, 2 * units - RES)
        def _(j):
            with jax.named_scope("Et"):
                dest, k = place(j, end, mid)
                total = take(dest, k, 1, j)
                add_squares(total)

                @pl.when(j < units)
                def _():
                    acc[dest, *unit(k)] = total

                @pl.when(j == 1)
                def _():
                    hello(0)

                @pl.when(j == units // 2)
                def _():
                    heard(0)
                    hello(1)

        heard(1)

    @pl.when(jnp.logical_not(at_end))
    def _():
        own_act(far_end).wait()
        own_vg(0).wait()
        for part in range(2):
            pair_act(far_end, part).wait_recv()
            pair_vg(0, part).wait_recv()
        for slot in range(heads):
            with jax.named_scope(f"Mm{slot}"):
                if slot:
                    ready_vg(slot)
                multiply(far_end, slot)
        for dest in order[1:]:
            ready(dest)

        def onward(j):
            dest, k = place(j, end, mid)
            total = take(dest, k, 1, j)

            @pl.when(j < 2 * units - RES)
            def _():
                give(total, dest, k, 1, j, behind)

            @pl.when(j >= units)
            def _():
                acc[dest, *unit(k)] = total

        @pl.loop(0, 2 * units)
        def _(i):
            with jax.named_scope("Mn"):
                dest, k = place(i, far_end, far_mid)
                give(take(dest, k, 0, i), dest, k, 1, i, ahead)

            @pl.when(i < 3 * heads)
            def _():
                dest = jnp.where(i < heads, end, jnp.where(i < 2 * heads, far_mid, mid))
                multiply(dest, lax.rem(i, heads))

            @pl.when(i >= LAG)
            def _():
                with jax.named_scope("Mf"):
                    onward(i - LAG)

            @pl.when(i == LAG + 1)
            def _():
                hello(0)

            @pl.when(i == LAG + units // 2)
            def _():
                heard(0)
                hello(1)

        @pl.loop(2 * units - LAG, 2 * units - RES)
        def _(j):
            with jax.named_scope("Mf"):
                onward(j)

        @pl.loop(0, RES)
        def _(k):
            with jax.named_scope("Mr"):
                onward(2 * units - RES + k)
                total = take(mid, k, 0, 2 * units + k)
                acc[mid, *unit(k)] = total
                add_squares(total)

        heard(1)

    me = dp * heads + mp
    norms[me] = jnp.sum(squares[...], axis=0, keepdims=True)

    def norm_to(step, slot):
        return pltpu.make_async_remote_copy(
            src_ref=norms.at[me],
            dst_ref=norms.at[me],
            send_sem=norm_sem.at[0],
            recv_sem=norm_sem.at[1],
            device_id={"dp": lax.rem(dp + step, dpn), "mp": lax.rem(mp + slot, heads)},
            device_id_type=MESH,
        )

    def taken(ref, sem):
        pltpu.make_async_copy(ref, ref, sem).wait()

    others = [(step, slot) for step in range(dpn) for slot in range(heads) if step + slot]
    with jax.named_scope("ns"):
        for step, slot in others:
            norm_to(step, slot).start()

    @pl.when(at_end)
    def _():
        @pl.loop(2 * units + RES + EARLY, 3 * units)
        def _(i):
            send(i)

    for copy in loads:
        copy.wait()
    with jax.named_scope("nw"):
        taken(norms.at[pl.ds(0, len(others))], norm_sem.at[1])
    square_sum = jnp.sum(jnp.sum(norms[...], axis=0), keepdims=True)
    factor = jnp.minimum(1.0, clip_total / (jnp.sqrt(square_sum) + 1e-06))
    step_count = jnp.full((1, 1), step_ref[0].astype(F32), F32)
    scale_first, scale_second = adam_terms(step_count)

    def block(owner, origin, part):
        start = (owner * dpn + origin) * rows + part * half
        return rollout_ref.at[pl.ds(pl.multiple_of(start, half), half)]

    def piece(head, part):
        return update.at[head, pl.ds(part * half, half)]

    def mine(part):
        return pltpu.make_async_copy(
            piece(mp, part), block(mp, dp, part), store_sem.at[3]
        )

    def to_head(slot, part):
        return pltpu.make_async_remote_copy(
            src_ref=piece(peer(slot), part),
            dst_ref=block(mp, dp, part),
            send_sem=a2a_send.at[0],
            recv_sem=a2a_recv.at[slot, part],
            device_id={"mp": peer(slot)},
            device_id_type=MESH,
        )

    def relay(ref, owner, at_z, part, send, recv, to):
        return pltpu.make_async_remote_copy(
            src_ref=ref,
            dst_ref=block(owner, at_z * 2 + core, part),
            send_sem=send,
            recv_sem=recv,
            device_id={"dp": to},
            device_id_type=MESH,
        )

    def send_ahead(ref, owner, at_z, part, sem=0):
        recv = chain_recv.at[at_z, owner, part]
        return relay(ref, owner, at_z, part, spread_send.at[sem], recv, ahead)

    def send_behind(ref, owner, at_z, part):
        recv = chain_recv.at[at_z, owner, part]
        return relay(ref, owner, at_z, part, spread_send.at[2], recv, behind)

    def send_mate(ref, owner, at_z, part):
        return relay(ref, owner, at_z, part, spread_send.at[3], mate_recv.at[0], mate)

    def spread(ref, owner, part):
        @pl.when(jnp.logical_not(at_end))
        def _():
            send_behind(ref, owner, z, part).start()

        send_ahead(ref, owner, z, part).start()
        send_mate(ref, owner, z, part).start()

    def from_ahead(at_z, slot, part):
        owner = source(slot)
        ref = block(owner, at_z * 2 + core, part)
        send_ahead(ref, owner, at_z, part).wait_recv()

        @pl.when(jnp.logical_not(at_end))
        def _():
            send_behind(ref, owner, at_z, part).start()

        send_mate(ref, owner, at_z, part).start()

    def from_behind(slot, part):
        owner = source(slot)
        ref = block(owner, end * 2 + core, part)
        send_ahead(ref, owner, end, part).wait_recv()
        send_ahead(ref, owner, end, part, 1).start()
        send_mate(ref, owner, end, part).start()

    def from_plane(slot, part):
        to_head(slot, part).wait_recv()
        spread(block(source(slot), dp, part), source(slot), part)

    slab = min(32, half)

    def step_rows(slot, part):
        lanes = head_lanes(slot)

        @pl.loop(0, half // slab)
        def _(r):
            at = pl.ds(pl.multiple_of(part * half + r * slab, slab), slab)
            clipped = acc[z, at, lanes] * factor
            weight = w_in[at, lanes]
            first = 0.9 * m_in[at, lanes] + 0.1 * clipped
            second = 0.95 * v_in[at, lanes] + 0.05 * clipped * clipped
            m_out[at, lanes] = first
            v_out[at, lanes] = second
            direction = (first * scale_first) / (
                jnp.sqrt(second * scale_second) + 1e-08
            ) + 0.1 * weight
            w_out[at, lanes] = weight - 0.01 * direction
            update[peer(slot), at, :] = direction.astype(jnp.bfloat16)

    def late(slot):
        @pl.when(jnp.logical_not(at_end))
        def _():
            @pl.loop(4 * slot, 4 * slot + 4)
            def _(k):
                acc[mid, *unit(k)] = take(mid, k, 0, 2 * units + k)

    work = [(slot, part) for slot in range(heads) for part in range(2)]
    for slot, part in work:
        with jax.named_scope(f"up{slot}{part}"):
            if part == 0 and 4 * slot >= RES:
                late(slot)
            step_rows(slot, part)
            if slot == 0:
                mine(part).start()
                spread(piece(mp, part), mp, part)
            else:
                to_head(slot, part).start()

    stores = [
        pltpu.make_async_copy(src, dst, store_sem.at[i])
        for i, (src, dst) in enumerate(
            ((w_out, new_master_ref), (m_out, new_first_ref), (v_out, new_second_ref))
        )
    ]
    for copy in stores:
        copy.start()

    @pl.when(at_end)
    def _():
        with jax.named_scope("Eaa"):
            for slot, part in work[2:]:
                from_plane(slot, part)
        for at_z in (mid, far_mid, far_end):
            with jax.named_scope("Efar"):
                for slot, part in work:
                    from_ahead(at_z, slot, part)

    @pl.when(jnp.logical_not(at_end))
    def _():
        for t, (slot, part) in enumerate(work[2:]):
            if t < 3:
                with jax.named_scope(f"Mah{t}"):
                    from_ahead(far_mid, *work[t])
            with jax.named_scope(f"Maa{t}"):
                from_plane(slot, part)
        for t in range(8):
            with jax.named_scope(f"Mfar{t}"):
                if t >= 3:
                    from_ahead(far_mid, *work[t])
                from_behind(*work[t])
        with jax.named_scope("Mfare"):
            for slot, part in work:
                from_ahead(far_end, slot, part)

    with jax.named_scope("tail"):
        plane = heads * rows
        taken(rollout_ref.at[pl.ds(0, line * plane)], mate_recv.at[0])
        taken(rollout_ref.at[pl.ds(0, line * plane)], spread_send.at[3])
        taken(rollout_ref.at[pl.ds(0, plane)], spread_send.at[0])

        @pl.when(jnp.logical_not(at_end))
        def _():
            taken(rollout_ref.at[pl.ds(0, plane)], spread_send.at[1])
            taken(rollout_ref.at[pl.ds(0, (line - 1) * plane)], spread_send.at[2])

        taken(update.at[pl.ds(0, heads - 1)], a2a_send.at[0])
        taken(norms.at[pl.ds(0, len(others))], norm_sem.at[0])
        taken(act.at[:, pl.ds(0, tokens)], pair_send.at[0])
        taken(vg.at[pl.ds(0, tokens)], pair_send.at[1])
        for i, ref in enumerate((q_out, s_out)):
            for dest in (far_end, far_mid):
                taken(ref.at[dest], rs_send.at[i, dest])

            @pl.when(at_end)
            def _():
                taken(ref.at[mid], rs_send.at[i, mid])

            @pl.when(jnp.logical_not(at_end))
            def _():
                taken(ref.at[end], rs_send.at[i, end])
                taken(ref.at[mid, pl.ds(RES, units - RES)], rs_send.at[i, mid])

        taken(update.at[0], store_sem.at[3])
        for copy in stores:
            copy.wait()


def settle(*refs):
    count = (len(refs) - 1) // 2
    sem = refs[-1]
    copies = []
    for i in range(count):
        source, place = refs[i], refs[count + i]
        piece = source.shape[0] // PIECES[i]
        for j in range(PIECES[i]):
            at = pl.ds(j * piece, piece)
            copies.append(
                pltpu.make_async_copy(source.at[at], place.at[at], sem.at[len(copies)])
            )
    for copy in copies:
        copy.start()
    for copy in copies:
        copy.wait()


def one_kernel(line, heads, activations, value_grad, master, first_moment, second_moment, step_count):
    rows, cols = master.shape
    tokens = activations.shape[0]
    tile = cols // heads // 2
    units = 4 * heads
    dpn = 2 * line
    clip_total = 0.5 * math.sqrt(rows * dpn * heads * cols)
    hbm = pl.BlockSpec(memory_space=pl.ANY)
    owned = jax.ShapeDtypeStruct((rows, cols), F32)
    wide = pltpu.VMEM((rows, cols), F32)
    dma = pltpu.SemaphoreType.DMA
    results = pl.pallas_call(
        functools.partial(kernel, line, heads, clip_total),
        out_shape=(
            owned,
            owned,
            owned,
            jax.ShapeDtypeStruct((rows * dpn * heads, cols // heads), jnp.bfloat16),
        ),
        in_specs=[pl.BlockSpec(memory_space=pltpu.SMEM)]
        + [hbm] * 5,
        out_specs=(hbm,) * 4,
        scratch_shapes=[
            pltpu.VMEM((line, 2 * tokens, rows), jnp.bfloat16),
            pltpu.VMEM((2 * tokens, cols), jnp.bfloat16),
            pltpu.VMEM((line, rows, cols), F32),
            pltpu.VMEM((line, units, rows // 2, tile), jnp.int16),
            pltpu.VMEM((line, units, 1, tile), F32),
            pltpu.VMEM((2, line, units, rows // 2, tile), jnp.int16),
            pltpu.VMEM((2, line, units, 1, tile), F32),
            pltpu.VMEM((8, tile), F32),
            pltpu.VMEM((dpn * heads, 1, tile), F32),
            pltpu.VMEM((rows // 4 + 1, 1, tile), F32),
            wide,
            wide,
            wide,
            wide,
            wide,
            wide,
            pltpu.VMEM((heads, rows, cols // heads), jnp.bfloat16),
            dma((line + heads,)),
            dma((2,)),
            dma((line + heads + 2,)),
            dma((3,)),
            dma((2, line)),
            dma((3 * units,)),
            dma((2 * units,)),
            pltpu.SemaphoreType.REGULAR((2,)),
            dma((2,)),
            dma((4,)),
            dma((1,)),
            dma((heads, 2)),
            dma((4,)),
            dma((line, heads, 2)),
            dma((1,)),
        ],
        compiler_params=pltpu.CompilerParams(
            collective_id=0, has_side_effects=True, vmem_limit_bytes=28 * 1024 * 1024
        ),
    )(
        step_count,
        *(
            pltpu.with_memory_space_constraint(x, pltpu.HBM)
            for x in (activations, value_grad, master, first_moment, second_moment)
        ),
    )
    shapes = tuple(jax.ShapeDtypeStruct(x.shape, x.dtype) for x in results)
    return pl.pallas_call(
        settle,
        out_shape=shapes,
        in_specs=[hbm] * 4,
        out_specs=(hbm,) * 4,
        scratch_shapes=[dma((sum(PIECES),))],
        compiler_params=pltpu.CompilerParams(vmem_limit_bytes=4 * 1024 * 1024),
    )(*(pltpu.with_memory_space_constraint(x, pltpu.VMEM) for x in results))


def plain(activations, value_grad, master, first_moment, second_moment, step_count):
    own_rows, cols = master.shape
    grad = lax.psum_scatter(
        lax.dot_general(
            activations, value_grad, (((0,), (0,)), ((), ())), preferred_element_type=F32
        ),
        "dp",
        scatter_dimension=0,
        tiled=True,
    )
    square_sum = lax.psum(jnp.sum(grad * grad), ("dp", "mp"))
    head_count = lax.axis_size("mp")
    clip_total = 0.5 * math.sqrt(own_rows * lax.axis_size("dp") * head_count * cols)
    factor = jnp.minimum(jnp.float32(1.0), clip_total / (jnp.sqrt(square_sum) + 1e-06))
    clipped = factor * grad
    new_first = 0.9 * first_moment + 0.1 * clipped
    new_second = 0.95 * second_moment + 0.05 * clipped * clipped
    scale_first, scale_second = adam_terms(step_count[0].astype(F32))
    direction = new_first * scale_first / (jnp.sqrt(new_second * scale_second) + 1e-08) + 0.1 * master
    new_master = master - 0.01 * direction
    update = direction.astype(jnp.bfloat16)
    received = lax.all_to_all(update, "mp", split_axis=1, concat_axis=0, tiled=True)
    stacked = received.reshape(head_count, own_rows, received.shape[1])
    gathered = lax.all_gather(stacked, "dp", axis=1, tiled=True)
    return (new_master, new_first, new_second, gathered.reshape(-1, gathered.shape[2]))


def solution(mesh):
    dpn, heads = mesh.shape["dp"], mesh.shape["mp"]

    def on_device(*args):
        rows, cols = args[2].shape
        if dpn == 8 and heads == 4 and rows % 64 == 0 and (cols // heads) % 256 == 0:
            return one_kernel(dpn // 2, heads, *args)
        return plain(*args)

    in_specs = (
        P("dp", "mp"),
        P("dp", None),
        P(("mp", "dp"), None),
        P(("mp", "dp"), None),
        P(("mp", "dp"), None),
        P(),
    )
    out_specs = (P(("mp", "dp"), None), P(("mp", "dp"), None), P(("mp", "dp"), None), P(None, "mp"))
    return jax.shard_map(
        on_device, mesh=mesh, in_specs=in_specs, out_specs=out_specs, check_vma=False
    )
```

```python
import functools
import math

import jax
import jax.numpy as jnp
from jax import lax
from jax.experimental import pallas as pl
from jax.experimental.pallas import tpu as pltpu
from jax.sharding import PartitionSpec as P

F32 = jnp.float32
LEVELS = 32760.0
PIECES = (1, 1, 1, 4)
RES = 4
LAG = 4
EARLY = 4
SHADOW = 3
BEFORE = 5
MESH = pl.DeviceIdType.MESH


def adam_terms(step):
    bias_first = 1.0 - jnp.exp(step * jnp.float32(math.log(0.9)))
    bias_second = 1.0 - jnp.exp(step * jnp.float32(math.log(0.95)))
    return 1.0 / bias_first, 1.0 / bias_second


def kernel(
    line,
    heads,
    clip_total,
    step_ref,
    act_ref,
    vg_ref,
    master_ref,
    first_ref,
    second_ref,
    new_master_ref,
    new_first_ref,
    new_second_ref,
    rollout_ref,
    act,
    vg,
    acc,
    q_out,
    s_out,
    q_in,
    s_in,
    squares,
    norms,
    tally,
    w_in,
    m_in,
    v_in,
    w_out,
    m_out,
    v_out,
    update,
    shadow_q,
    shadow_s,
    in_sem,
    pair_send,
    pair_recv,
    load_sem,
    rs_send,
    near_recv,
    wide_recv,
    meet,
    norm_sem,
    shadow_sem,
    a2a_send,
    mate_recv,
):
    dpn = 2 * line
    dp = lax.axis_index("dp")
    mp = lax.axis_index("mp")
    z = dp // 2
    core = lax.rem(dp, 2)
    mate = dp + 1 - 2 * core
    tokens = act_ref.shape[0]
    rows = master_ref.shape[0]
    cols = master_ref.shape[1]
    head_cols = cols // heads
    tile = head_cols // 2
    half = rows // 2
    units = 4 * heads
    blocks = 2 * heads

    lower = z < line // 2
    at_end = (z == 0) | (z == line - 1)
    end = jnp.where(lower, 0, line - 1)
    mid = jnp.where(lower, 1, line - 2)
    far_mid = line - 1 - mid
    far_end = line - 1 - end
    toward = jnp.where(lower, 2, -2)
    ahead = dp + toward
    behind = jnp.where(at_end, dp, dp - toward)

    def peer(slot):
        return lax.rem(mp // 2 + slot // 2, heads // 2) * 2 + lax.rem(mp + slot % 2, 2)

    def source(slot):
        y = lax.rem(mp // 2 + heads // 2 - slot // 2, heads // 2)
        return y * 2 + lax.rem(mp + slot % 2, 2)

    barrier = pltpu.get_barrier_semaphore()
    pl.semaphore_signal(barrier, inc=1, device_id={"dp": mate}, device_id_type=MESH)
    pl.semaphore_signal(barrier, inc=1, device_id={"dp": ahead}, device_id_type=MESH)

    @pl.when(jnp.logical_not(at_end))
    def _():
        pl.semaphore_signal(barrier, inc=1, device_id={"dp": behind}, device_id_type=MESH)

    for slot in (1, 2):
        pl.semaphore_signal(barrier, inc=1, device_id={"mp": peer(slot)}, device_id_type=MESH)

    def own_act(dest):
        start = pl.multiple_of((dest * 2 + core) * rows, rows)
        return pltpu.make_async_copy(
            act_ref.at[:, pl.ds(start, rows)],
            act.at[dest, pl.ds(0, tokens)],
            in_sem.at[dest],
        )

    def head_lanes(slot):
        return pl.ds(pl.multiple_of(peer(slot) * head_cols, head_cols), head_cols)

    def chunk_lanes(k):
        at = peer(k // 2) * 2 + k % 2
        return pl.ds(pl.multiple_of(at * tile, tile), tile)

    def unit(k):
        return pl.ds(pl.multiple_of(k % 2 * half, half), half), chunk_lanes(k // 2)

    def own_vg(slot):
        at = head_lanes(slot)
        return pltpu.make_async_copy(
            vg_ref.at[:, at], vg.at[pl.ds(0, tokens), at], in_sem.at[line + slot]
        )

    def pair_act(dest, part=None):
        at = part or 0
        count = rows if part is None else half
        start = pl.multiple_of((dest * 2 + 1 - core) * rows + at * half, half)
        return pltpu.make_async_remote_copy(
            src_ref=act_ref.at[:, pl.ds(start, count)],
            dst_ref=act.at[dest, pl.ds(tokens, tokens), pl.ds(at * half, count)],
            send_sem=pair_send.at[0],
            recv_sem=pair_recv.at[line if part else dest],
            device_id={"dp": mate},
            device_id_type=MESH,
        )

    def pair_vg(slot, part=None):
        at = head_lanes(slot) if part is None else chunk_lanes(2 * slot + part)
        return pltpu.make_async_remote_copy(
            src_ref=vg_ref.at[:, at],
            dst_ref=vg.at[pl.ds(tokens, tokens), at],
            send_sem=pair_send.at[1],
            recv_sem=pair_recv.at[line + 1 + (heads if part else slot)],
            device_id={"dp": mate},
            device_id_type=MESH,
        )

    order = [
        far_end,
        jnp.where(at_end, far_mid, end),
        jnp.where(at_end, mid, far_mid),
        jnp.where(at_end, end, mid),
    ]
    own_act(order[0]).start()
    for slot in range(heads):
        own_vg(slot).start()
    for dest in order[1:]:
        own_act(dest).start()
    loads = [
        pltpu.make_async_copy(src, dst, load_sem.at[i])
        for i, (src, dst) in enumerate(
            ((master_ref, w_in), (first_ref, m_in), (second_ref, v_in))
        )
    ]
    for copy in loads:
        copy.start()
    with jax.named_scope("bar"):
        pl.semaphore_wait(barrier, jnp.where(at_end, 4, 5))
    for part in range(2):
        pair_act(order[0], part).start()
        pair_vg(0, part).start()
    for slot in range(1, heads):
        pair_vg(slot).start()
    for dest in order[1:]:
        pair_act(dest).start()

    def ready(dest):
        own_act(dest).wait()
        pair_act(dest).wait_recv()

    def ready_vg(slot):
        own_vg(slot).wait()
        pair_vg(slot).wait_recv()

    def multiply_unit(dest, part, k):
        at = chunk_lanes(k)
        here = slice(part * half, (part + 1) * half)
        acc[dest, here, at] = lax.dot_general(
            act[dest, :, here], vg[:, at], (((0,), (0,)), ((), ())), preferred_element_type=F32
        )

    def multiply(dest, slot):
        at = head_lanes(slot)
        acc[dest, :, at] = lax.dot_general(
            act[dest], vg[:, at], (((0,), (0,)), ((), ())), preferred_element_type=F32
        )

    def hop(dest, k, way, i, to):
        recv = (near_recv, wide_recv)[way]
        data = pltpu.make_async_remote_copy(
            src_ref=q_out.at[dest, k],
            dst_ref=q_in.at[way, dest, k],
            send_sem=rs_send.at[0, dest],
            recv_sem=recv.at[i],
            device_id={"dp": to},
            device_id_type=MESH,
        )
        scale = pltpu.make_async_remote_copy(
            src_ref=s_out.at[dest, k],
            dst_ref=s_in.at[way, dest, k],
            send_sem=rs_send.at[1, dest],
            recv_sem=recv.at[i],
            device_id={"dp": to},
            device_id_type=MESH,
        )
        return data, scale

    def arrived(way, i):
        pltpu.make_async_copy(tally, tally, (near_recv, wide_recv)[way].at[i]).wait()

    def take(dest, k, way, i):
        arrived(way, i)
        return acc[dest, *unit(k)] + decode(q_in[way, dest, k], s_in[way, dest, k])

    def code(total):
        top = jnp.maximum(jnp.max(jnp.abs(total), axis=0, keepdims=True), 1e-30)
        return jnp.round(total * (LEVELS / top)).astype(jnp.int32).astype(jnp.int16), top

    def decode(got, top):
        return got.astype(jnp.int32).astype(F32) * (top * (1.0 / LEVELS))

    def give(total, dest, k, way, i, to):
        q_out[dest, k], s_out[dest, k] = code(total)
        for copy in hop(dest, k, way, i, to):
            copy.start()

    def add_squares(total):
        squares[...] += jnp.sum((total * total).reshape(half // 8, 8, tile), axis=0)

    def place(i, first, second):
        dest = jnp.where(i < units, first, second)
        return dest, jnp.where(i < units, i, lax.rem(i + RES, units))

    def shadowed(k):
        return k // 4 * 2 + k % 2 >= blocks - SHADOW

    def lend(first, last):
        for at in range(first, last):
            t, i = blocks - SHADOW + at // 3, at % 3
            here = slice(t % 2 * half, (t % 2 + 1) * half)
            value = (m_in, v_in, w_in)[i][here, head_lanes(t // 2)]
            shadow_q[i, at // 3], shadow_s[i, at // 3] = code(value)
            for j, ref in enumerate((shadow_q, shadow_s)):
                pltpu.make_async_remote_copy(
                    src_ref=ref.at[i, at // 3],
                    dst_ref=ref.at[i, at // 3],
                    send_sem=shadow_sem.at[j],
                    recv_sem=shadow_sem.at[2 + j],
                    device_id={"dp": behind},
                    device_id_type=MESH,
                ).start()

    squares[...] = jnp.zeros(squares.shape, F32)

    def hello(stage):
        slot = stage + 1
        pl.semaphore_signal(
            meet.at[stage], inc=1, device_id={"mp": peer(slot)}, device_id_type=MESH
        )

    def heard(stage):
        pl.semaphore_wait(meet.at[stage], 1)

    def send(i):
        dest, k = place(i, far_end, far_mid)
        dest = jnp.where(i < 2 * units, dest, mid)
        k = jnp.where(i < 2 * units, k, i - 2 * units)
        give(acc[dest, *unit(k)], dest, k, 0, i, ahead)

    @pl.when(at_end)
    def _():
        own_act(far_end).wait()
        own_vg(0).wait()
        for k in range(2):
            for part in range(2):
                with jax.named_scope(f"Ew{k}{part}"):
                    if k == 0:
                        pair_act(far_end, part).wait_recv()
                    if part == 0:
                        pair_vg(0, k).wait_recv()
                with jax.named_scope(f"Em{k}{part}"):
                    multiply_unit(far_end, part, k)
                    send(2 * k + part)

        for slot in range(1, heads):
            with jax.named_scope(f"Em{slot}"):
                ready_vg(slot)
                multiply(far_end, slot)
                for k in range(4):
                    send(4 * slot + k)

        with jax.named_scope("Erest"):
            ready(far_mid)

            @pl.loop(0, heads)
            def _(slot):
                multiply(far_mid, slot)

            @pl.loop(units, 2 * units)
            def _(i):
                send(i)

            ready(mid)

            @pl.loop(0, heads)
            def _(slot):
                multiply(mid, slot)

            @pl.loop(2 * units, 2 * units + RES + EARLY)
            def _(i):
                send(i)

            ready(end)

            @pl.loop(0, heads)
            def _(slot):
                multiply(end, slot)

        @pl.loop(0, 2 * units - RES)
        def _(j):
            with jax.named_scope("Et"):
                dest, k = place(j, end, mid)
                total = take(dest, k, 1, j)
                add_squares(total)

                @pl.when(j < units)
                def _():
                    acc[dest, *unit(k)] = total

                @pl.when((j >= units) & shadowed(k))
                def _():
                    q, top = code(total)
                    q_out[mid, k], s_out[mid, k] = q, top
                    q_in[0, mid, k], s_in[0, mid, k] = q, top

                @pl.when(j == 1)
                def _():
                    hello(0)

                @pl.when(j == units // 2)
                def _():
                    heard(0)
                    hello(1)

        heard(1)

    @pl.when(jnp.logical_not(at_end))
    def _():
        with jax.named_scope("Ml"):
            for copy in loads:
                copy.wait()
            lend(0, BEFORE)
        own_act(far_end).wait()
        own_vg(0).wait()
        for part in range(2):
            pair_act(far_end, part).wait_recv()
            pair_vg(0, part).wait_recv()
        for slot in range(heads):
            with jax.named_scope(f"Mm{slot}"):
                if slot:
                    ready_vg(slot)
                multiply(far_end, slot)
        for dest in order[1:]:
            ready(dest)

        def onward(j):
            dest, k = place(j, end, mid)
            total = take(dest, k, 1, j)

            @pl.when(j < 2 * units - RES)
            def _():
                give(total, dest, k, 1, j, behind)

            @pl.when(j >= units)
            def _():
                acc[dest, *unit(k)] = total

        @pl.loop(0, 2 * units)
        def _(i):
            with jax.named_scope("Mn"):
                dest, k = place(i, far_end, far_mid)
                give(take(dest, k, 0, i), dest, k, 1, i, ahead)

            @pl.when(i < 3 * heads)
            def _():
                dest = jnp.where(i < heads, end, jnp.where(i < 2 * heads, far_mid, mid))
                multiply(dest, lax.rem(i, heads))

            @pl.when(i >= LAG)
            def _():
                with jax.named_scope("Mf"):
                    onward(i - LAG)

            @pl.when(i == LAG + 1)
            def _():
                hello(0)

            @pl.when(i == LAG + units // 2)
            def _():
                heard(0)
                hello(1)

        @pl.loop(2 * units - LAG, 2 * units - RES)
        def _(j):
            with jax.named_scope("Mf"):
                onward(j)

        @pl.loop(0, RES)
        def _(k):
            with jax.named_scope("Mr"):
                onward(2 * units - RES + k)
                total = take(mid, k, 0, 2 * units + k)
                acc[mid, *unit(k)] = total
                add_squares(total)

        heard(1)

    me = dp * heads + mp
    norms[me] = jnp.sum(squares[...], axis=0, keepdims=True)

    def norm_to(step, slot):
        return pltpu.make_async_remote_copy(
            src_ref=norms.at[me],
            dst_ref=norms.at[me],
            send_sem=norm_sem.at[0],
            recv_sem=norm_sem.at[1],
            device_id={"dp": lax.rem(dp + step, dpn), "mp": lax.rem(mp + slot, heads)},
            device_id_type=MESH,
        )

    def taken(ref, sem):
        pltpu.make_async_copy(ref, ref, sem).wait()

    others = [(step, slot) for step in range(dpn) for slot in range(heads) if step + slot]
    with jax.named_scope("ns"):
        for step, slot in others:
            norm_to(step, slot).start()

    @pl.when(at_end)
    def _():
        @pl.loop(2 * units + RES + EARLY, 3 * units)
        def _(i):
            k = i - 2 * units

            @pl.when(shadowed(k))
            def _():
                for copy in hop(mid, k, 0, i, ahead):
                    copy.start()

            @pl.when(jnp.logical_not(shadowed(k)))
            def _():
                send(i)

        for copy in loads:
            copy.wait()

    @pl.when(jnp.logical_not(at_end))
    def _():
        with jax.named_scope("Ml2"):
            lend(BEFORE, 3 * SHADOW)

    with jax.named_scope("nw"):
        taken(norms.at[pl.ds(0, len(others))], norm_sem.at[1])
    square_sum = jnp.sum(jnp.sum(norms[...], axis=0), keepdims=True)
    factor = jnp.minimum(1.0, clip_total / (jnp.sqrt(square_sum) + 1e-06))
    step_count = jnp.full((1, 1), step_ref[0].astype(F32), F32)
    scale_first, scale_second = adam_terms(step_count)

    def block(owner, origin, part):
        start = (owner * dpn + origin) * rows + part * half
        return rollout_ref.at[pl.ds(pl.multiple_of(start, half), half)]

    def piece(head, part):
        return update.at[head * 2 + part]

    def mine(part):
        return pltpu.make_async_copy(
            piece(mp, part), block(mp, dp, part), in_sem.at[line + 3]
        )

    def to_head(slot, part):
        return pltpu.make_async_remote_copy(
            src_ref=piece(peer(slot), part),
            dst_ref=block(mp, dp, part),
            send_sem=a2a_send.at[0],
            recv_sem=near_recv.at[slot * 2 + part],
            device_id={"mp": peer(slot)},
            device_id_type=MESH,
        )

    def to_shadow(at):
        t = blocks - SHADOW + at
        return pltpu.make_async_remote_copy(
            src_ref=update.at[blocks + at],
            dst_ref=block(mp, mid * 2 + core, t % 2),
            send_sem=shadow_sem.at[0],
            recv_sem=near_recv.at[blocks + at],
            device_id={"mp": peer(t // 2)},
            device_id_type=MESH,
        )

    def relay(ref, owner, at_z, part, send, recv, to):
        return pltpu.make_async_remote_copy(
            src_ref=ref,
            dst_ref=block(owner, at_z * 2 + core, part),
            send_sem=send,
            recv_sem=recv,
            device_id={"dp": to},
            device_id_type=MESH,
        )

    def send_ahead(ref, owner, at_z, part, sem=0):
        recv = wide_recv.at[(at_z * heads + owner) * 2 + part]
        return relay(ref, owner, at_z, part, in_sem.at[sem], recv, ahead)

    def send_behind(ref, owner, at_z, part):
        recv = wide_recv.at[(at_z * heads + owner) * 2 + part]
        return relay(ref, owner, at_z, part, in_sem.at[2], recv, behind)

    def send_mate(ref, owner, at_z, part):
        return relay(ref, owner, at_z, part, in_sem.at[3], mate_recv.at[0], mate)

    def spread(ref, owner, part, back=True):
        if back:

            @pl.when(jnp.logical_not(at_end))
            def _():
                send_behind(ref, owner, z, part).start()

        send_ahead(ref, owner, z, part).start()
        send_mate(ref, owner, z, part).start()

    def from_ahead(at_z, slot, part):
        owner = source(slot)
        ref = block(owner, at_z * 2 + core, part)
        send_ahead(ref, owner, at_z, part).wait_recv()

        @pl.when(jnp.logical_not(at_end))
        def _():
            send_behind(ref, owner, at_z, part).start()

        send_mate(ref, owner, at_z, part).start()

    def from_behind(slot, part):
        owner = source(slot)
        ref = block(owner, end * 2 + core, part)
        send_ahead(ref, owner, end, part).wait_recv()
        send_ahead(ref, owner, end, part, 1).start()
        send_mate(ref, owner, end, part).start()

    def from_plane(slot, part):
        to_head(slot, part).wait_recv()
        back = slot * 2 + part < blocks - SHADOW
        spread(block(source(slot), dp, part), source(slot), part, back)

    def from_shadow(at):
        t = blocks - SHADOW + at
        owner = source(t // 2)
        to_shadow(at).wait_recv()
        send_mate(block(owner, mid * 2 + core, t % 2), owner, mid, t % 2).start()

    slab = min(32, half)

    def step_rows(slot, part):
        lanes = head_lanes(slot)

        @pl.loop(0, half // slab)
        def _(r):
            at = pl.ds(pl.multiple_of(part * half + r * slab, slab), slab)
            clipped = acc[z, at, lanes] * factor
            weight = w_in[at, lanes]
            first = 0.9 * m_in[at, lanes] + 0.1 * clipped
            second = 0.95 * v_in[at, lanes] + 0.05 * clipped * clipped
            m_out[at, lanes] = first
            v_out[at, lanes] = second
            direction = (first * scale_first) / (
                jnp.sqrt(second * scale_second) + 1e-08
            ) + 0.1 * weight
            w_out[at, lanes] = weight - 0.01 * direction
            here = pl.ds(pl.multiple_of(r * slab, slab), slab)
            update[peer(slot) * 2 + part, here, :] = direction.astype(jnp.bfloat16)

    def shadow_rows(at):
        t = blocks - SHADOW + at
        slot, part = t // 2, t % 2
        to = jnp.where(at_end, blocks + at, peer(slot) * 2 + part)

        @pl.loop(0, half // slab)
        def _(r):
            here = pl.ds(pl.multiple_of(r * slab, slab), slab)
            for c in range(2):
                k = 4 * slot + 2 * c + part
                lanes = slice(c * tile, (c + 1) * tile)
                first, second, weight = (
                    decode(shadow_q[i, at, here, lanes], shadow_s[i, at, :, lanes])
                    for i in range(3)
                )
                clipped = decode(q_in[0, mid, k, here, :], s_in[0, mid, k]) * factor
                first = 0.9 * first + 0.1 * clipped
                second = 0.95 * second + 0.05 * clipped * clipped
                direction = (first * scale_first) / (
                    jnp.sqrt(second * scale_second) + 1e-08
                ) + 0.1 * weight
                update[to, here, lanes] = direction.astype(jnp.bfloat16)

    def late(slot):
        @pl.when(jnp.logical_not(at_end))
        def _():
            for k in range(max(4 * slot, RES), 4 * slot + 4):
                if shadowed(k):
                    arrived(0, 2 * units + k)
                    acc[mid, *unit(k)] = decode(q_in[0, mid, k], s_in[0, mid, k])
                else:
                    acc[mid, *unit(k)] = take(mid, k, 0, 2 * units + k)

    work = [(slot, part) for slot in range(heads) for part in range(2)]
    for slot, part in work:
        with jax.named_scope(f"up{slot}{part}"):
            at = slot * 2 + part - (blocks - SHADOW)
            if part == 0 and 4 * slot + 4 > RES:
                late(slot)
            step_rows(slot, part)
            if at >= 0:

                @pl.when(jnp.logical_not(at_end))
                def _():
                    shadow_rows(at)

            if slot == 0:
                mine(part).start()
                spread(piece(mp, part), mp, part)
            else:
                to_head(slot, part).start()

    stores = [
        pltpu.make_async_copy(src, dst, in_sem.at[line + i])
        for i, (src, dst) in enumerate(
            ((w_out, new_master_ref), (m_out, new_first_ref), (v_out, new_second_ref))
        )
    ]
    for copy in stores:
        copy.start()

    @pl.when(at_end)
    def _():
        with jax.named_scope("Es"):
            for j, ref in enumerate((shadow_q, shadow_s)):
                taken(ref, shadow_sem.at[2 + j])
            for at in range(SHADOW):
                shadow_rows(at)
                to_shadow(at).start()
        with jax.named_scope("Eaa"):
            for slot, part in work[2:]:
                from_plane(slot, part)
            for slot, part in work[: blocks - SHADOW]:
                from_ahead(mid, slot, part)
            for at in range(SHADOW):
                from_shadow(at)
        for at_z in (far_mid, far_end):
            with jax.named_scope("Efar"):
                for slot, part in work:
                    from_ahead(at_z, slot, part)

    @pl.when(jnp.logical_not(at_end))
    def _():
        for t, (slot, part) in enumerate(work[2:]):
            if t < 3:
                with jax.named_scope(f"Mah{t}"):
                    from_ahead(far_mid, *work[t])
            with jax.named_scope(f"Maa{t}"):
                from_plane(slot, part)
        for t in range(8):
            with jax.named_scope(f"Mfar{t}"):
                if t >= 3:
                    from_ahead(far_mid, *work[t])
                from_behind(*work[t])
        with jax.named_scope("Mfare"):
            for slot, part in work:
                from_ahead(far_end, slot, part)

    with jax.named_scope("tail"):
        plane = heads * rows
        taken(rollout_ref.at[pl.ds(0, line * plane)], mate_recv.at[0])
        taken(rollout_ref.at[pl.ds(0, line * plane)], in_sem.at[3])
        taken(rollout_ref.at[pl.ds(0, plane)], in_sem.at[0])

        @pl.when(jnp.logical_not(at_end))
        def _():
            taken(rollout_ref.at[pl.ds(0, plane)], in_sem.at[1])
            back = (line - 1) * plane - SHADOW * half
            taken(rollout_ref.at[pl.ds(0, back)], in_sem.at[2])
            for j, ref in enumerate((shadow_q, shadow_s)):
                taken(ref, shadow_sem.at[j])

        @pl.when(at_end)
        def _():
            taken(update.at[pl.ds(0, SHADOW)], shadow_sem.at[0])

        taken(update.at[pl.ds(0, blocks - 2)], a2a_send.at[0])
        taken(norms.at[pl.ds(0, len(others))], norm_sem.at[0])
        taken(act.at[:, pl.ds(0, tokens)], pair_send.at[0])
        taken(vg.at[pl.ds(0, tokens)], pair_send.at[1])
        for i, ref in enumerate((q_out, s_out)):
            for dest in (far_end, far_mid):
                taken(ref.at[dest], rs_send.at[i, dest])

            @pl.when(at_end)
            def _():
                taken(ref.at[mid], rs_send.at[i, mid])

            @pl.when(jnp.logical_not(at_end))
            def _():
                taken(ref.at[end], rs_send.at[i, end])
                taken(ref.at[mid, pl.ds(RES, units - RES)], rs_send.at[i, mid])

        taken(update.at[pl.ds(0, 2)], in_sem.at[line + 3])
        for copy in stores:
            copy.wait()


def settle(*refs):
    count = (len(refs) - 1) // 2
    sem = refs[-1]
    copies = []
    for i in range(count):
        source, place = refs[i], refs[count + i]
        piece = source.shape[0] // PIECES[i]
        for j in range(PIECES[i]):
            at = pl.ds(j * piece, piece)
            copies.append(
                pltpu.make_async_copy(source.at[at], place.at[at], sem.at[len(copies)])
            )
    for copy in copies:
        copy.start()
    for copy in copies:
        copy.wait()


def one_kernel(line, heads, activations, value_grad, master, first_moment, second_moment, step_count):
    rows, cols = master.shape
    tokens = activations.shape[0]
    tile = cols // heads // 2
    units = 4 * heads
    dpn = 2 * line
    clip_total = 0.5 * math.sqrt(rows * dpn * heads * cols)
    hbm = pl.BlockSpec(memory_space=pl.ANY)
    owned = jax.ShapeDtypeStruct((rows, cols), F32)
    wide = pltpu.VMEM((rows, cols), F32)
    dma = pltpu.SemaphoreType.DMA
    results = pl.pallas_call(
        functools.partial(kernel, line, heads, clip_total),
        out_shape=(
            owned,
            owned,
            owned,
            jax.ShapeDtypeStruct((rows * dpn * heads, cols // heads), jnp.bfloat16),
        ),
        in_specs=[pl.BlockSpec(memory_space=pltpu.SMEM)]
        + [hbm] * 5,
        out_specs=(hbm,) * 4,
        scratch_shapes=[
            pltpu.VMEM((line, 2 * tokens, rows), jnp.bfloat16),
            pltpu.VMEM((2 * tokens, cols), jnp.bfloat16),
            pltpu.VMEM((line, rows, cols), F32),
            pltpu.VMEM((line, units, rows // 2, tile), jnp.int16),
            pltpu.VMEM((line, units, 1, tile), F32),
            pltpu.VMEM((2, line, units, rows // 2, tile), jnp.int16),
            pltpu.VMEM((2, line, units, 1, tile), F32),
            pltpu.VMEM((8, tile), F32),
            pltpu.VMEM((dpn * heads, 1, tile), F32),
            pltpu.VMEM((rows // 4 + 1, 1, tile), F32),
            wide,
            wide,
            wide,
            wide,
            wide,
            wide,
            pltpu.VMEM((2 * heads + SHADOW, rows // 2, 2 * tile), jnp.bfloat16),
            pltpu.VMEM((3, SHADOW, rows // 2, 2 * tile), jnp.int16),
            pltpu.VMEM((3, SHADOW, 1, 2 * tile), F32),
            dma((line + heads,)),
            dma((2,)),
            dma((line + heads + 2,)),
            dma((3,)),
            dma((2, line)),
            dma((3 * units,)),
            dma((2 * units,)),
            pltpu.SemaphoreType.REGULAR((2,)),
            dma((2,)),
            dma((4,)),
            dma((1,)),
            dma((1,)),
        ],
        compiler_params=pltpu.CompilerParams(
            collective_id=0, has_side_effects=True, vmem_limit_bytes=28 * 1024 * 1024
        ),
    )(
        step_count,
        *(
            pltpu.with_memory_space_constraint(x, pltpu.HBM)
            for x in (activations, value_grad, master, first_moment, second_moment)
        ),
    )
    shapes = tuple(jax.ShapeDtypeStruct(x.shape, x.dtype) for x in results)
    return pl.pallas_call(
        settle,
        out_shape=shapes,
        in_specs=[hbm] * 4,
        out_specs=(hbm,) * 4,
        scratch_shapes=[dma((sum(PIECES),))],
        compiler_params=pltpu.CompilerParams(vmem_limit_bytes=4 * 1024 * 1024),
    )(*(pltpu.with_memory_space_constraint(x, pltpu.VMEM) for x in results))


def plain(activations, value_grad, master, first_moment, second_moment, step_count):
    own_rows, cols = master.shape
    grad = lax.psum_scatter(
        lax.dot_general(
            activations, value_grad, (((0,), (0,)), ((), ())), preferred_element_type=F32
        ),
        "dp",
        scatter_dimension=0,
        tiled=True,
    )
    square_sum = lax.psum(jnp.sum(grad * grad), ("dp", "mp"))
    head_count = lax.axis_size("mp")
    clip_total = 0.5 * math.sqrt(own_rows * lax.axis_size("dp") * head_count * cols)
    factor = jnp.minimum(jnp.float32(1.0), clip_total / (jnp.sqrt(square_sum) + 1e-06))
    clipped = factor * grad
    new_first = 0.9 * first_moment + 0.1 * clipped
    new_second = 0.95 * second_moment + 0.05 * clipped * clipped
    scale_first, scale_second = adam_terms(step_count[0].astype(F32))
    direction = new_first * scale_first / (jnp.sqrt(new_second * scale_second) + 1e-08) + 0.1 * master
    new_master = master - 0.01 * direction
    update = direction.astype(jnp.bfloat16)
    received = lax.all_to_all(update, "mp", split_axis=1, concat_axis=0, tiled=True)
    stacked = received.reshape(head_count, own_rows, received.shape[1])
    gathered = lax.all_gather(stacked, "dp", axis=1, tiled=True)
    return (new_master, new_first, new_second, gathered.reshape(-1, gathered.shape[2]))


def solution(mesh):
    dpn, heads = mesh.shape["dp"], mesh.shape["mp"]

    def on_device(*args):
        rows, cols = args[2].shape
        if dpn == 8 and heads == 4 and rows % 64 == 0 and (cols // heads) % 256 == 0:
            return one_kernel(dpn // 2, heads, *args)
        return plain(*args)

    in_specs = (
        P("dp", "mp"),
        P("dp", None),
        P(("mp", "dp"), None),
        P(("mp", "dp"), None),
        P(("mp", "dp"), None),
        P(),
    )
    out_specs = (P(("mp", "dp"), None), P(("mp", "dp"), None), P(("mp", "dp"), None), P(None, "mp"))
    return jax.shard_map(
        on_device, mesh=mesh, in_specs=in_specs, out_specs=out_specs, check_vma=False
    )
```

```python
import functools
import math

import jax
import jax.numpy as jnp
from jax import lax
from jax.experimental import pallas as pl
from jax.experimental.pallas import tpu as pltpu
from jax.sharding import PartitionSpec as P

F32 = jnp.float32
LEVELS = 32760.0
PIECES = (1, 1, 1, 4)
RES = 5
LAG = 5
EARLY = 3
SHADOW = 3
LENT = (5, 7)
ROOT_MID = (1.0 + math.sqrt(0.05)) / 2
ROOT_SPAN = (1.0 - math.sqrt(0.05)) / 2
MESH = pl.DeviceIdType.MESH


def adam_terms(step):
    bias_first = 1.0 - jnp.exp(step * jnp.float32(math.log(0.9)))
    bias_second = 1.0 - jnp.exp(step * jnp.float32(math.log(0.95)))
    return 1.0 / bias_first, 1.0 / bias_second


def kernel(
    line,
    heads,
    clip_total,
    step_ref,
    act_ref,
    vg_ref,
    master_ref,
    first_ref,
    second_ref,
    new_master_ref,
    new_first_ref,
    new_second_ref,
    rollout_ref,
    act,
    vg,
    acc,
    q_out,
    s_out,
    q_in,
    s_in,
    squares,
    norms,
    tally,
    w_in,
    m_in,
    v_in,
    w_out,
    m_out,
    v_out,
    update,
    shadow_q,
    shadow_s,
    in_sem,
    pair_send,
    pair_recv,
    load_sem,
    rs_send,
    near_recv,
    wide_recv,
    meet,
    norm_sem,
    shadow_sem,
    a2a_send,
    mate_recv,
):
    dpn = 2 * line
    dp = lax.axis_index("dp")
    mp = lax.axis_index("mp")
    z = dp // 2
    core = lax.rem(dp, 2)
    mate = dp + 1 - 2 * core
    tokens = act_ref.shape[0]
    rows = master_ref.shape[0]
    cols = master_ref.shape[1]
    head_cols = cols // heads
    tile = head_cols // 2
    half = rows // 2
    units = 4 * heads
    blocks = 2 * heads

    lower = z < line // 2
    at_end = (z == 0) | (z == line - 1)
    end = jnp.where(lower, 0, line - 1)
    mid = jnp.where(lower, 1, line - 2)
    far_mid = line - 1 - mid
    far_end = line - 1 - end
    toward = jnp.where(lower, 2, -2)
    ahead = dp + toward
    behind = jnp.where(at_end, dp, dp - toward)

    def peer(slot):
        return lax.rem(mp // 2 + slot // 2, heads // 2) * 2 + lax.rem(mp + slot % 2, 2)

    def source(slot):
        y = lax.rem(mp // 2 + heads // 2 - slot // 2, heads // 2)
        return y * 2 + lax.rem(mp + slot % 2, 2)

    barrier = pltpu.get_barrier_semaphore()
    pl.semaphore_signal(barrier, inc=1, device_id={"dp": mate}, device_id_type=MESH)
    pl.semaphore_signal(barrier, inc=1, device_id={"dp": ahead}, device_id_type=MESH)

    @pl.when(jnp.logical_not(at_end))
    def _():
        pl.semaphore_signal(barrier, inc=1, device_id={"dp": behind}, device_id_type=MESH)

    for slot in (1, 2):
        pl.semaphore_signal(barrier, inc=1, device_id={"mp": peer(slot)}, device_id_type=MESH)

    def own_act(dest):
        start = pl.multiple_of((dest * 2 + core) * rows, rows)
        return pltpu.make_async_copy(
            act_ref.at[:, pl.ds(start, rows)],
            act.at[dest, pl.ds(0, tokens)],
            in_sem.at[dest],
        )

    def head_lanes(slot):
        return pl.ds(pl.multiple_of(peer(slot) * head_cols, head_cols), head_cols)

    def chunk_lanes(k):
        at = peer(k // 2) * 2 + k % 2
        return pl.ds(pl.multiple_of(at * tile, tile), tile)

    def unit(k):
        return pl.ds(pl.multiple_of(k % 2 * half, half), half), chunk_lanes(k // 2)

    def own_vg(slot):
        at = head_lanes(slot)
        return pltpu.make_async_copy(
            vg_ref.at[:, at], vg.at[pl.ds(0, tokens), at], in_sem.at[line + slot]
        )

    def pair_act(dest, part=None):
        at = part or 0
        count = rows if part is None else half
        start = pl.multiple_of((dest * 2 + 1 - core) * rows + at * half, half)
        return pltpu.make_async_remote_copy(
            src_ref=act_ref.at[:, pl.ds(start, count)],
            dst_ref=act.at[dest, pl.ds(tokens, tokens), pl.ds(at * half, count)],
            send_sem=pair_send.at[0],
            recv_sem=pair_recv.at[line if part else dest],
            device_id={"dp": mate},
            device_id_type=MESH,
        )

    def pair_vg(slot, part=None):
        at = head_lanes(slot) if part is None else chunk_lanes(2 * slot + part)
        return pltpu.make_async_remote_copy(
            src_ref=vg_ref.at[:, at],
            dst_ref=vg.at[pl.ds(tokens, tokens), at],
            send_sem=pair_send.at[1],
            recv_sem=pair_recv.at[line + 1 + (heads if part else slot)],
            device_id={"dp": mate},
            device_id_type=MESH,
        )

    order = [
        far_end,
        jnp.where(at_end, far_mid, end),
        jnp.where(at_end, mid, far_mid),
        jnp.where(at_end, end, mid),
    ]
    own_act(order[0]).start()
    for slot in range(heads):
        own_vg(slot).start()
    for dest in order[1:]:
        own_act(dest).start()
    loads = [
        pltpu.make_async_copy(src, dst, load_sem.at[i])
        for i, (src, dst) in enumerate(
            ((master_ref, w_in), (first_ref, m_in), (second_ref, v_in))
        )
    ]
    with jax.named_scope("bar"):
        pl.semaphore_wait(barrier, jnp.where(at_end, 4, 5))
    for part in range(2):
        pair_act(order[0], part).start()
        pair_vg(0, part).start()
    @pl.when(jnp.logical_not(at_end))
    def _():
        for copy in loads:
            copy.start()

    for slot in range(1, heads):
        pair_vg(slot).start()
    for dest in order[1:]:
        pair_act(dest).start()

    def ready(dest):
        own_act(dest).wait()
        pair_act(dest).wait_recv()

    def ready_vg(slot):
        own_vg(slot).wait()
        pair_vg(slot).wait_recv()

    def multiply_unit(dest, part, k, mates):
        at = chunk_lanes(k)
        here = slice(part * half, (part + 1) * half)
        whose = slice(mates * tokens, (mates + 1) * tokens)
        product = lax.dot_general(
            act[dest, whose, here],
            vg[whose, at],
            (((0,), (0,)), ((), ())),
            preferred_element_type=F32,
        )
        acc[dest, here, at] = acc[dest, here, at] + product if mates else product

    def multiply(dest, slot):
        at = head_lanes(slot)
        acc[dest, :, at] = lax.dot_general(
            act[dest], vg[:, at], (((0,), (0,)), ((), ())), preferred_element_type=F32
        )

    def hop(dest, k, way, i, to):
        recv = (near_recv, wide_recv)[way]
        data = pltpu.make_async_remote_copy(
            src_ref=q_out.at[dest, k],
            dst_ref=q_in.at[way, dest, k],
            send_sem=rs_send.at[0, dest],
            recv_sem=recv.at[i],
            device_id={"dp": to},
            device_id_type=MESH,
        )
        scale = pltpu.make_async_remote_copy(
            src_ref=s_out.at[dest, k],
            dst_ref=s_in.at[way, dest, k],
            send_sem=rs_send.at[1, dest],
            recv_sem=recv.at[i],
            device_id={"dp": to},
            device_id_type=MESH,
        )
        return data, scale

    def arrived(way, i):
        pltpu.make_async_copy(tally, tally, (near_recv, wide_recv)[way].at[i]).wait()

    def take(dest, k, way, i):
        arrived(way, i)
        return acc[dest, *unit(k)] + decode(q_in[way, dest, k], s_in[way, dest, k])

    def code(total):
        top = jnp.maximum(jnp.max(jnp.abs(total), axis=0, keepdims=True), 1e-30)
        return jnp.round(total * (LEVELS / top)).astype(jnp.int32).astype(jnp.int16), top

    def decode(got, top):
        return got.astype(jnp.int32).astype(F32) * (top * (1.0 / LEVELS))

    def give(total, dest, k, way, i, to):
        q_out[dest, k], s_out[dest, k] = code(total)
        for copy in hop(dest, k, way, i, to):
            copy.start()

    def add_squares(total):
        squares[...] += jnp.sum((total * total).reshape(half // 8, 8, tile), axis=0)

    def place(i, first, second):
        dest = jnp.where(i < units, first, second)
        return dest, jnp.where(i < units, i, lax.rem(i + RES, units))

    def shadowed(k):
        return k // 4 * 2 + k % 2 >= blocks - SHADOW

    def lend(first, last):
        for at in range(first, last):
            n, i = at // 3, at % 3
            t = blocks - SHADOW + n
            here = slice(t % 2 * half, (t % 2 + 1) * half)
            value = (m_in, w_in, v_in)[i][here, head_lanes(t // 2)]
            refs = [shadow_q]
            if i < 2:
                shadow_q[i, n], shadow_s[i, n] = code(value)
                refs.append(shadow_s)
            else:
                root = (jnp.sqrt(value) - ROOT_MID) * (LEVELS / ROOT_SPAN)
                shadow_q[i, n] = jnp.round(root).astype(jnp.int32).astype(jnp.int16)
            for j, ref in enumerate(refs):
                pltpu.make_async_remote_copy(
                    src_ref=ref.at[i, n],
                    dst_ref=ref.at[i, n],
                    send_sem=shadow_sem.at[j],
                    recv_sem=shadow_sem.at[2 + j],
                    device_id={"dp": behind},
                    device_id_type=MESH,
                ).start()

    squares[...] = jnp.zeros(squares.shape, F32)

    def hello(stage):
        slot = stage + 1
        pl.semaphore_signal(
            meet.at[stage], inc=1, device_id={"mp": peer(slot)}, device_id_type=MESH
        )

    def heard(stage):
        pl.semaphore_wait(meet.at[stage], 1)

    def send(i):
        dest, k = place(i, far_end, far_mid)
        dest = jnp.where(i < 2 * units, dest, mid)
        k = jnp.where(i < 2 * units, k, i - 2 * units)
        give(acc[dest, *unit(k)], dest, k, 0, i, ahead)

    @pl.when(at_end)
    def _():
        own_act(far_end).wait()
        own_vg(0).wait()
        for k in range(2):
            for part in range(2):
                multiply_unit(far_end, part, k, 0)
        for k in range(2):
            for part in range(2):
                with jax.named_scope(f"Ew{k}{part}"):
                    if k == 0:
                        pair_act(far_end, part).wait_recv()
                    if part == 0:
                        pair_vg(0, k).wait_recv()
                with jax.named_scope(f"Em{k}{part}"):
                    multiply_unit(far_end, part, k, 1)
                    send(2 * k + part)

        for slot in range(1, heads):
            with jax.named_scope(f"Em{slot}"):
                ready_vg(slot)
                multiply(far_end, slot)
                for k in range(4):
                    send(4 * slot + k)

        for copy in loads:
            copy.start()
        with jax.named_scope("Erest"):
            ready(far_mid)

            @pl.loop(0, heads)
            def _(slot):
                multiply(far_mid, slot)

            @pl.loop(units, 2 * units)
            def _(i):
                send(i)

            ready(mid)

            @pl.loop(0, heads)
            def _(slot):
                multiply(mid, slot)

            @pl.loop(2 * units, 2 * units + RES + EARLY)
            def _(i):
                send(i)

            ready(end)

            @pl.loop(0, heads)
            def _(slot):
                multiply(end, slot)

        @pl.loop(0, 2 * units - RES)
        def _(j):
            with jax.named_scope("Et"):
                dest, k = place(j, end, mid)
                total = take(dest, k, 1, j)
                add_squares(total)

                @pl.when(j < units)
                def _():
                    acc[dest, *unit(k)] = total

                @pl.when((j >= units) & shadowed(k))
                def _():
                    q, top = code(total)
                    q_out[mid, k], s_out[mid, k] = q, top
                    q_in[0, mid, k], s_in[0, mid, k] = q, top

                @pl.when(j == 1)
                def _():
                    hello(0)

                @pl.when(j == units // 2)
                def _():
                    heard(0)
                    hello(1)

        heard(1)

    @pl.when(jnp.logical_not(at_end))
    def _():
        with jax.named_scope("Ml"):
            for copy in loads:
                copy.wait()
            lend(0, LENT[0])
        own_act(far_end).wait()
        own_vg(0).wait()
        for part in range(2):
            pair_act(far_end, part).wait_recv()
            pair_vg(0, part).wait_recv()
        for slot in range(heads):
            with jax.named_scope(f"Mm{slot}"):
                if slot:
                    ready_vg(slot)
                multiply(far_end, slot)
        for dest in order[1:]:
            ready(dest)

        def onward(j):
            dest, k = place(j, end, mid)
            total = take(dest, k, 1, j)

            @pl.when(j < 2 * units - RES)
            def _():
                give(total, dest, k, 1, j, behind)

            @pl.when(j >= units)
            def _():
                acc[dest, *unit(k)] = total

        @pl.loop(0, 2 * units)
        def _(i):
            with jax.named_scope("Mn"):
                dest, k = place(i, far_end, far_mid)
                give(take(dest, k, 0, i), dest, k, 1, i, ahead)

            @pl.when(i < 3 * heads)
            def _():
                dest = jnp.where(i < heads, end, jnp.where(i < 2 * heads, far_mid, mid))
                multiply(dest, lax.rem(i, heads))

            @pl.when(i >= LAG)
            def _():
                with jax.named_scope("Mf"):
                    onward(i - LAG)

            @pl.when(i == LAG + 1)
            def _():
                hello(0)

            @pl.when(i == LAG + units // 2)
            def _():
                heard(0)
                hello(1)

        @pl.loop(2 * units - LAG, 2 * units - RES)
        def _(j):
            with jax.named_scope("Mf"):
                onward(j)

        lend(*LENT)

        @pl.loop(0, RES)
        def _(k):
            with jax.named_scope("Mr"):
                onward(2 * units - RES + k)
                total = take(mid, k, 0, 2 * units + k)
                acc[mid, *unit(k)] = total
                add_squares(total)

        heard(1)

    me = dp * heads + mp
    norms[me] = jnp.sum(squares[...], axis=0, keepdims=True)

    def norm_to(at_z, other, slot):
        return pltpu.make_async_remote_copy(
            src_ref=norms.at[me],
            dst_ref=norms.at[me],
            send_sem=norm_sem.at[0],
            recv_sem=norm_sem.at[1],
            device_id={"dp": at_z * 2 + lax.rem(core + other, 2), "mp": peer(slot)},
            device_id_type=MESH,
        )

    def taken(ref, sem):
        pltpu.make_async_copy(ref, ref, sem).wait()

    others = [
        (at_z, other, slot)
        for i, at_z in enumerate((far_end, far_mid, jnp.where(at_end, mid, end), z))
        for slot in range(heads - 1, -1, -1)
        for other in (1, 0)
        if i < 3 or other or slot
    ]
    with jax.named_scope("ns"):
        for at in others:
            norm_to(*at).start()

    @pl.when(at_end)
    def _():
        @pl.loop(2 * units + RES + EARLY, 3 * units)
        def _(i):
            k = i - 2 * units

            @pl.when(shadowed(k))
            def _():
                for copy in hop(mid, k, 0, i, ahead):
                    copy.start()

            @pl.when(jnp.logical_not(shadowed(k)))
            def _():
                send(i)

        for copy in loads:
            copy.wait()

    @pl.when(jnp.logical_not(at_end))
    def _():
        with jax.named_scope("Ml2"):
            lend(LENT[1], 3 * SHADOW)

    with jax.named_scope("nw"):
        taken(norms.at[pl.ds(0, len(others))], norm_sem.at[1])
    square_sum = jnp.sum(jnp.sum(norms[...], axis=0), keepdims=True)
    factor = jnp.minimum(1.0, clip_total / (jnp.sqrt(square_sum) + 1e-06))
    step_count = jnp.full((1, 1), step_ref[0].astype(F32), F32)
    scale_first, scale_second = adam_terms(step_count)

    def block(owner, origin, part):
        start = (owner * dpn + origin) * rows + part * half
        return rollout_ref.at[pl.ds(pl.multiple_of(start, half), half)]

    def piece(head, part):
        return update.at[head * 2 + part]

    def mine(part):
        return pltpu.make_async_copy(
            piece(mp, part), block(mp, dp, part), in_sem.at[line + 3]
        )

    def to_head(slot, part):
        return pltpu.make_async_remote_copy(
            src_ref=piece(peer(slot), part),
            dst_ref=block(mp, dp, part),
            send_sem=a2a_send.at[0],
            recv_sem=near_recv.at[slot * 2 + part],
            device_id={"mp": peer(slot)},
            device_id_type=MESH,
        )

    def to_shadow(at):
        t = blocks - SHADOW + at
        return pltpu.make_async_remote_copy(
            src_ref=update.at[blocks + at],
            dst_ref=block(mp, mid * 2 + core, t % 2),
            send_sem=shadow_sem.at[0],
            recv_sem=near_recv.at[blocks + at],
            device_id={"mp": peer(t // 2)},
            device_id_type=MESH,
        )

    def relay(ref, owner, at_z, part, send, recv, to):
        return pltpu.make_async_remote_copy(
            src_ref=ref,
            dst_ref=block(owner, at_z * 2 + core, part),
            send_sem=send,
            recv_sem=recv,
            device_id={"dp": to},
            device_id_type=MESH,
        )

    def send_ahead(ref, owner, at_z, part, sem=0):
        recv = wide_recv.at[(at_z * heads + owner) * 2 + part]
        return relay(ref, owner, at_z, part, in_sem.at[sem], recv, ahead)

    def send_behind(ref, owner, at_z, part):
        recv = wide_recv.at[(at_z * heads + owner) * 2 + part]
        return relay(ref, owner, at_z, part, in_sem.at[2], recv, behind)

    def send_mate(ref, owner, at_z, part):
        return relay(ref, owner, at_z, part, in_sem.at[3], mate_recv.at[0], mate)

    def spread(ref, owner, part, back=True):
        if back:

            @pl.when(jnp.logical_not(at_end))
            def _():
                send_behind(ref, owner, z, part).start()

        send_ahead(ref, owner, z, part).start()
        send_mate(ref, owner, z, part).start()

    def spread_slab(r):
        here = pl.ds(r * slab, slab)
        start = pl.multiple_of((mp * dpn + dp) * rows + r * slab, slab)
        recv = wide_recv.at[(z * heads + mp) * 2]

        def copy(i, recv, to):
            return pltpu.make_async_remote_copy(
                src_ref=update.at[mp * 2, here],
                dst_ref=rollout_ref.at[pl.ds(start, slab)],
                send_sem=in_sem.at[i],
                recv_sem=recv,
                device_id={"dp": to},
                device_id_type=MESH,
            )

        @pl.when(jnp.logical_not(at_end))
        def _():
            copy(2, recv, behind).start()

        copy(0, recv, ahead).start()
        copy(3, mate_recv.at[0], mate).start()

    def from_ahead(at_z, slot, part):
        owner = source(slot)
        ref = block(owner, at_z * 2 + core, part)
        send_ahead(ref, owner, at_z, part).wait_recv()

        @pl.when(jnp.logical_not(at_end))
        def _():
            send_behind(ref, owner, at_z, part).start()

        send_mate(ref, owner, at_z, part).start()

    def from_behind(slot, part):
        owner = source(slot)
        ref = block(owner, end * 2 + core, part)
        send_ahead(ref, owner, end, part).wait_recv()
        send_ahead(ref, owner, end, part, 1).start()
        send_mate(ref, owner, end, part).start()

    def from_plane(slot, part):
        to_head(slot, part).wait_recv()
        back = slot * 2 + part < blocks - SHADOW
        spread(block(source(slot), dp, part), source(slot), part, back)

    def from_shadow(at):
        t = blocks - SHADOW + at
        owner = source(t // 2)
        to_shadow(at).wait_recv()
        send_mate(block(owner, mid * 2 + core, t % 2), owner, mid, t % 2).start()

    slab = min(32, half)

    def step_rows(slot, part, first=0, last=half // slab):
        lanes = head_lanes(slot)

        @pl.loop(first, last)
        def _(r):
            at = pl.ds(pl.multiple_of(part * half + r * slab, slab), slab)
            clipped = acc[z, at, lanes] * factor
            weight = w_in[at, lanes]
            first = 0.9 * m_in[at, lanes] + 0.1 * clipped
            second = 0.95 * v_in[at, lanes] + 0.05 * clipped * clipped
            m_out[at, lanes] = first
            v_out[at, lanes] = second
            direction = (first * scale_first) / (
                jnp.sqrt(second * scale_second) + 1e-08
            ) + 0.1 * weight
            w_out[at, lanes] = weight - 0.01 * direction
            here = pl.ds(pl.multiple_of(r * slab, slab), slab)
            update[peer(slot) * 2 + part, here, :] = direction.astype(jnp.bfloat16)

    def shadow_rows(at):
        t = blocks - SHADOW + at
        slot, part = t // 2, t % 2
        to = jnp.where(at_end, blocks + at, peer(slot) * 2 + part)

        @pl.loop(0, half // slab)
        def _(r):
            here = pl.ds(pl.multiple_of(r * slab, slab), slab)
            for c in range(2):
                k = 4 * slot + 2 * c + part
                lanes = slice(c * tile, (c + 1) * tile)
                first, weight = (
                    decode(shadow_q[i, at, here, lanes], shadow_s[i, at, :, lanes])
                    for i in range(2)
                )
                root = shadow_q[2, at, here, lanes].astype(jnp.int32).astype(F32)
                root = root * (ROOT_SPAN / LEVELS) + ROOT_MID
                second = root * root
                clipped = decode(q_in[0, mid, k, here, :], s_in[0, mid, k]) * factor
                first = 0.9 * first + 0.1 * clipped
                second = 0.95 * second + 0.05 * clipped * clipped
                direction = (first * scale_first) / (
                    jnp.sqrt(second * scale_second) + 1e-08
                ) + 0.1 * weight
                update[to, here, lanes] = direction.astype(jnp.bfloat16)

    def late(slot):
        @pl.when(jnp.logical_not(at_end))
        def _():
            for k in range(max(4 * slot, RES), 4 * slot + 4):
                if shadowed(k):
                    arrived(0, 2 * units + k)
                    acc[mid, *unit(k)] = decode(q_in[0, mid, k], s_in[0, mid, k])
                else:
                    acc[mid, *unit(k)] = take(mid, k, 0, 2 * units + k)

    work = [(slot, part) for slot in range(heads) for part in range(2)]
    for slot, part in work:
        with jax.named_scope(f"up{slot}{part}"):
            at = slot * 2 + part - (blocks - SHADOW)
            if part == 0 and 4 * slot + 4 > RES:
                late(slot)
            if slot + part == 0:
                for r in range(half // slab):
                    step_rows(0, 0, r, r + 1)
                    spread_slab(r)
            else:
                step_rows(slot, part)
            if at >= 0:

                @pl.when(jnp.logical_not(at_end))
                def _():
                    shadow_rows(at)

            if slot == 0:
                mine(part).start()
                if part:
                    spread(piece(mp, part), mp, part)
            else:
                to_head(slot, part).start()

    stores = [
        pltpu.make_async_copy(src, dst, in_sem.at[line + i])
        for i, (src, dst) in enumerate(
            ((w_out, new_master_ref), (m_out, new_first_ref), (v_out, new_second_ref))
        )
    ]
    for copy in stores:
        copy.start()

    @pl.when(at_end)
    def _():
        with jax.named_scope("Es"):
            for j, ref in enumerate((shadow_q, shadow_s)):
                taken(ref, shadow_sem.at[2 + j])
            for at in range(SHADOW):
                shadow_rows(at)
                to_shadow(at).start()
        with jax.named_scope("Eaa"):
            for slot, part in work[2:]:
                from_plane(slot, part)
            for slot, part in work[: blocks - SHADOW]:
                from_ahead(mid, slot, part)
            for at in range(SHADOW):
                from_shadow(at)
        for at_z in (far_mid, far_end):
            with jax.named_scope("Efar"):
                for slot, part in work:
                    from_ahead(at_z, slot, part)

    @pl.when(jnp.logical_not(at_end))
    def _():
        for t, (slot, part) in enumerate(work[2:]):
            if t < 3:
                with jax.named_scope(f"Mah{t}"):
                    from_ahead(far_mid, *work[t])
            with jax.named_scope(f"Maa{t}"):
                from_plane(slot, part)
        for t in range(8):
            with jax.named_scope(f"Mfar{t}"):
                if t >= 3:
                    from_ahead(far_mid, *work[t])
                from_behind(*work[t])
        with jax.named_scope("Mfare"):
            for slot, part in work:
                from_ahead(far_end, slot, part)

    with jax.named_scope("tail"):
        plane = heads * rows
        taken(rollout_ref.at[pl.ds(0, line * plane)], mate_recv.at[0])
        taken(rollout_ref.at[pl.ds(0, line * plane)], in_sem.at[3])
        taken(rollout_ref.at[pl.ds(0, plane)], in_sem.at[0])

        @pl.when(jnp.logical_not(at_end))
        def _():
            taken(rollout_ref.at[pl.ds(0, plane)], in_sem.at[1])
            back = (line - 1) * plane - SHADOW * half
            taken(rollout_ref.at[pl.ds(0, back)], in_sem.at[2])
            for j, ref in enumerate((shadow_q, shadow_s)):
                taken(ref, shadow_sem.at[j])

        @pl.when(at_end)
        def _():
            taken(update.at[pl.ds(0, SHADOW)], shadow_sem.at[0])

        taken(update.at[pl.ds(0, blocks - 2)], a2a_send.at[0])
        taken(norms.at[pl.ds(0, len(others))], norm_sem.at[0])
        taken(act.at[:, pl.ds(0, tokens)], pair_send.at[0])
        taken(vg.at[pl.ds(0, tokens)], pair_send.at[1])
        for i, ref in enumerate((q_out, s_out)):
            for dest in (far_end, far_mid):
                taken(ref.at[dest], rs_send.at[i, dest])

            @pl.when(at_end)
            def _():
                taken(ref.at[mid], rs_send.at[i, mid])

            @pl.when(jnp.logical_not(at_end))
            def _():
                taken(ref.at[end], rs_send.at[i, end])
                taken(ref.at[mid, pl.ds(RES, units - RES)], rs_send.at[i, mid])

        taken(update.at[pl.ds(0, 2)], in_sem.at[line + 3])
        for copy in stores:
            copy.wait()


def settle(*refs):
    count = (len(refs) - 1) // 2
    sem = refs[-1]
    copies = []
    for i in range(count):
        source, place = refs[i], refs[count + i]
        piece = source.shape[0] // PIECES[i]
        for j in range(PIECES[i]):
            at = pl.ds(j * piece, piece)
            copies.append(
                pltpu.make_async_copy(source.at[at], place.at[at], sem.at[len(copies)])
            )
    for copy in copies:
        copy.start()
    for copy in copies:
        copy.wait()


def one_kernel(line, heads, activations, value_grad, master, first_moment, second_moment, step_count):
    rows, cols = master.shape
    tokens = activations.shape[0]
    tile = cols // heads // 2
    units = 4 * heads
    dpn = 2 * line
    clip_total = 0.5 * math.sqrt(rows * dpn * heads * cols)
    hbm = pl.BlockSpec(memory_space=pl.ANY)
    owned = jax.ShapeDtypeStruct((rows, cols), F32)
    wide = pltpu.VMEM((rows, cols), F32)
    dma = pltpu.SemaphoreType.DMA
    results = pl.pallas_call(
        functools.partial(kernel, line, heads, clip_total),
        out_shape=(
            owned,
            owned,
            owned,
            jax.ShapeDtypeStruct((rows * dpn * heads, cols // heads), jnp.bfloat16),
        ),
        in_specs=[pl.BlockSpec(memory_space=pltpu.SMEM)] + [hbm] * 5,
        out_specs=(hbm,) * 4,
        scratch_shapes=[
            pltpu.VMEM((line, 2 * tokens, rows), jnp.bfloat16),
            pltpu.VMEM((2 * tokens, cols), jnp.bfloat16),
            pltpu.VMEM((line, rows, cols), F32),
            pltpu.VMEM((line, units, rows // 2, tile), jnp.int16),
            pltpu.VMEM((line, units, 1, tile), F32),
            pltpu.VMEM((2, line, units, rows // 2, tile), jnp.int16),
            pltpu.VMEM((2, line, units, 1, tile), F32),
            pltpu.VMEM((8, tile), F32),
            pltpu.VMEM((dpn * heads, 1, tile), F32),
            pltpu.VMEM((rows // 4 + 1, 1, tile), F32),
            wide,
            wide,
            wide,
            wide,
            wide,
            wide,
            pltpu.VMEM((2 * heads + SHADOW, rows // 2, 2 * tile), jnp.bfloat16),
            pltpu.VMEM((3, SHADOW, rows // 2, 2 * tile), jnp.int16),
            pltpu.VMEM((2, SHADOW, 1, 2 * tile), F32),
            dma((line + heads,)),
            dma((2,)),
            dma((line + heads + 2,)),
            dma((3,)),
            dma((2, line)),
            dma((3 * units,)),
            dma((2 * units,)),
            pltpu.SemaphoreType.REGULAR((2,)),
            dma((2,)),
            dma((4,)),
            dma((1,)),
            dma((1,)),
        ],
        compiler_params=pltpu.CompilerParams(
            collective_id=0, has_side_effects=True, vmem_limit_bytes=28 * 1024 * 1024
        ),
    )(
        step_count,
        *(
            pltpu.with_memory_space_constraint(x, pltpu.HBM)
            for x in (activations, value_grad, master, first_moment, second_moment)
        ),
    )
    shapes = tuple(jax.ShapeDtypeStruct(x.shape, x.dtype) for x in results)
    return pl.pallas_call(
        settle,
        out_shape=shapes,
        in_specs=[hbm] * 4,
        out_specs=(hbm,) * 4,
        scratch_shapes=[dma((sum(PIECES),))],
        compiler_params=pltpu.CompilerParams(vmem_limit_bytes=4 * 1024 * 1024),
    )(*(pltpu.with_memory_space_constraint(x, pltpu.VMEM) for x in results))


def plain(activations, value_grad, master, first_moment, second_moment, step_count):
    own_rows, cols = master.shape
    grad = lax.psum_scatter(
        lax.dot_general(
            activations, value_grad, (((0,), (0,)), ((), ())), preferred_element_type=F32
        ),
        "dp",
        scatter_dimension=0,
        tiled=True,
    )
    square_sum = lax.psum(jnp.sum(grad * grad), ("dp", "mp"))
    head_count = lax.axis_size("mp")
    clip_total = 0.5 * math.sqrt(own_rows * lax.axis_size("dp") * head_count * cols)
    factor = jnp.minimum(jnp.float32(1.0), clip_total / (jnp.sqrt(square_sum) + 1e-06))
    clipped = factor * grad
    new_first = 0.9 * first_moment + 0.1 * clipped
    new_second = 0.95 * second_moment + 0.05 * clipped * clipped
    scale_first, scale_second = adam_terms(step_count[0].astype(F32))
    direction = new_first * scale_first / (jnp.sqrt(new_second * scale_second) + 1e-08) + 0.1 * master
    new_master = master - 0.01 * direction
    update = direction.astype(jnp.bfloat16)
    received = lax.all_to_all(update, "mp", split_axis=1, concat_axis=0, tiled=True)
    stacked = received.reshape(head_count, own_rows, received.shape[1])
    gathered = lax.all_gather(stacked, "dp", axis=1, tiled=True)
    return (new_master, new_first, new_second, gathered.reshape(-1, gathered.shape[2]))


def solution(mesh):
    dpn, heads = mesh.shape["dp"], mesh.shape["mp"]

    def on_device(*args):
        rows, cols = args[2].shape
        if dpn == 8 and heads == 4 and rows % 64 == 0 and (cols // heads) % 256 == 0:
            return one_kernel(dpn // 2, heads, *args)
        return plain(*args)

    in_specs = (
        P("dp", "mp"),
        P("dp", None),
        P(("mp", "dp"), None),
        P(("mp", "dp"), None),
        P(("mp", "dp"), None),
        P(),
    )
    out_specs = (P(("mp", "dp"), None), P(("mp", "dp"), None), P(("mp", "dp"), None), P(None, "mp"))
    return jax.shard_map(
        on_device, mesh=mesh, in_specs=in_specs, out_specs=out_specs, check_vma=False
    )
```

```python
import functools
import math

import jax
import jax.numpy as jnp
from jax import lax
from jax.experimental import pallas as pl
from jax.experimental.pallas import tpu as pltpu
from jax.sharding import PartitionSpec as P

F32 = jnp.float32
LEVELS = 32760.0
PIECES = (1, 1, 1, 4)
RES = 5
LAG = 4
EARLY = 3
SHADOW = 3
LENT = (4, 7)
ROOT_MID = (1.0 + math.sqrt(0.05)) / 2
ROOT_SPAN = (1.0 - math.sqrt(0.05)) / 2
MESH = pl.DeviceIdType.MESH


def adam_terms(step):
    bias_first = 1.0 - jnp.exp(step * jnp.float32(math.log(0.9)))
    bias_second = 1.0 - jnp.exp(step * jnp.float32(math.log(0.95)))
    return 1.0 / bias_first, 1.0 / bias_second


def kernel(
    line,
    heads,
    clip_total,
    step_ref,
    act_ref,
    vg_ref,
    master_ref,
    first_ref,
    second_ref,
    new_master_ref,
    new_first_ref,
    new_second_ref,
    rollout_ref,
    act,
    vg,
    acc,
    q_out,
    s_out,
    q_in,
    s_in,
    squares,
    norms,
    tally,
    w_in,
    m_in,
    v_in,
    w_out,
    m_out,
    v_out,
    update,
    shadow_q,
    shadow_s,
    in_sem,
    pair_send,
    pair_recv,
    load_sem,
    rs_send,
    near_recv,
    wide_recv,
    meet,
    norm_sem,
    shadow_sem,
    a2a_send,
    mate_recv,
):
    dpn = 2 * line
    dp = lax.axis_index("dp")
    mp = lax.axis_index("mp")
    z = dp // 2
    core = lax.rem(dp, 2)
    mate = dp + 1 - 2 * core
    tokens = act_ref.shape[0]
    rows = master_ref.shape[0]
    cols = master_ref.shape[1]
    head_cols = cols // heads
    tile = head_cols // 2
    half = rows // 2
    units = 4 * heads
    blocks = 2 * heads

    lower = z < line // 2
    at_end = (z == 0) | (z == line - 1)
    end = jnp.where(lower, 0, line - 1)
    mid = jnp.where(lower, 1, line - 2)
    far_mid = line - 1 - mid
    far_end = line - 1 - end
    toward = jnp.where(lower, 2, -2)
    ahead = dp + toward
    behind = jnp.where(at_end, dp, dp - toward)

    def peer(slot):
        return lax.rem(mp // 2 + slot // 2, heads // 2) * 2 + lax.rem(mp + slot % 2, 2)

    def source(slot):
        y = lax.rem(mp // 2 + heads // 2 - slot // 2, heads // 2)
        return y * 2 + lax.rem(mp + slot % 2, 2)

    barrier = pltpu.get_barrier_semaphore()
    pl.semaphore_signal(barrier, inc=1, device_id={"dp": mate}, device_id_type=MESH)
    pl.semaphore_signal(barrier, inc=1, device_id={"dp": ahead}, device_id_type=MESH)

    @pl.when(jnp.logical_not(at_end))
    def _():
        pl.semaphore_signal(barrier, inc=1, device_id={"dp": behind}, device_id_type=MESH)

    for slot in (1, 2):
        pl.semaphore_signal(barrier, inc=1, device_id={"mp": peer(slot)}, device_id_type=MESH)

    def own_act(dest):
        start = pl.multiple_of((dest * 2 + core) * rows, rows)
        return pltpu.make_async_copy(
            act_ref.at[:, pl.ds(start, rows)],
            act.at[dest, pl.ds(0, tokens)],
            in_sem.at[dest],
        )

    def head_lanes(slot):
        return pl.ds(pl.multiple_of(peer(slot) * head_cols, head_cols), head_cols)

    def chunk_lanes(k):
        at = peer(k // 2) * 2 + k % 2
        return pl.ds(pl.multiple_of(at * tile, tile), tile)

    def unit(k):
        return pl.ds(pl.multiple_of(k % 2 * half, half), half), chunk_lanes(k // 2)

    def own_vg(slot):
        at = head_lanes(slot)
        return pltpu.make_async_copy(
            vg_ref.at[:, at], vg.at[pl.ds(0, tokens), at], in_sem.at[line + slot]
        )

    def pair_act(dest, part=None):
        at = part or 0
        count = rows if part is None else half
        start = pl.multiple_of((dest * 2 + 1 - core) * rows + at * half, half)
        return pltpu.make_async_remote_copy(
            src_ref=act_ref.at[:, pl.ds(start, count)],
            dst_ref=act.at[dest, pl.ds(tokens, tokens), pl.ds(at * half, count)],
            send_sem=pair_send.at[0],
            recv_sem=pair_recv.at[line if part else dest],
            device_id={"dp": mate},
            device_id_type=MESH,
        )

    def pair_vg(slot, part=None):
        at = head_lanes(slot) if part is None else chunk_lanes(2 * slot + part)
        return pltpu.make_async_remote_copy(
            src_ref=vg_ref.at[:, at],
            dst_ref=vg.at[pl.ds(tokens, tokens), at],
            send_sem=pair_send.at[1],
            recv_sem=pair_recv.at[line + 1 + (heads if part else slot)],
            device_id={"dp": mate},
            device_id_type=MESH,
        )

    order = [
        far_end,
        jnp.where(at_end, far_mid, end),
        jnp.where(at_end, mid, far_mid),
        jnp.where(at_end, end, mid),
    ]
    own_act(order[0]).start()
    for slot in range(heads):
        own_vg(slot).start()
    for dest in order[1:]:
        own_act(dest).start()
    loads = [
        pltpu.make_async_copy(src, dst, load_sem.at[i])
        for i, (src, dst) in enumerate(
            ((master_ref, w_in), (first_ref, m_in), (second_ref, v_in))
        )
    ]
    with jax.named_scope("bar"):
        pl.semaphore_wait(barrier, jnp.where(at_end, 4, 5))
    for part in range(2):
        pair_act(order[0], part).start()
        pair_vg(0, part).start()
    @pl.when(jnp.logical_not(at_end))
    def _():
        for copy in loads:
            copy.start()

    for slot in range(1, heads):
        pair_vg(slot).start()
    for dest in order[1:]:
        pair_act(dest).start()

    def ready(dest):
        own_act(dest).wait()
        pair_act(dest).wait_recv()

    def ready_vg(slot):
        own_vg(slot).wait()
        pair_vg(slot).wait_recv()

    def multiply_unit(dest, part, k, mates):
        at = chunk_lanes(k)
        here = slice(part * half, (part + 1) * half)
        whose = slice(mates * tokens, (mates + 1) * tokens)
        product = lax.dot_general(
            act[dest, whose, here],
            vg[whose, at],
            (((0,), (0,)), ((), ())),
            preferred_element_type=F32,
        )
        acc[dest, here, at] = acc[dest, here, at] + product if mates else product

    def multiply(dest, slot):
        at = head_lanes(slot)
        acc[dest, :, at] = lax.dot_general(
            act[dest], vg[:, at], (((0,), (0,)), ((), ())), preferred_element_type=F32
        )

    def hop(dest, k, way, i, to):
        recv = (near_recv, wide_recv)[way]
        data = pltpu.make_async_remote_copy(
            src_ref=q_out.at[dest, k],
            dst_ref=q_in.at[way, dest, k],
            send_sem=rs_send.at[0, dest],
            recv_sem=recv.at[i],
            device_id={"dp": to},
            device_id_type=MESH,
        )
        scale = pltpu.make_async_remote_copy(
            src_ref=s_out.at[dest, k],
            dst_ref=s_in.at[way, dest, k],
            send_sem=rs_send.at[1, dest],
            recv_sem=recv.at[i],
            device_id={"dp": to},
            device_id_type=MESH,
        )
        return data, scale

    def arrived(way, i):
        pltpu.make_async_copy(tally, tally, (near_recv, wide_recv)[way].at[i]).wait()

    def take(dest, k, way, i):
        arrived(way, i)
        return acc[dest, *unit(k)] + decode(q_in[way, dest, k], s_in[way, dest, k])

    def code(total):
        top = jnp.maximum(jnp.max(jnp.abs(total), axis=0, keepdims=True), 1e-30)
        return jnp.round(total * (LEVELS / top)).astype(jnp.int32).astype(jnp.int16), top

    def decode(got, top):
        return got.astype(jnp.int32).astype(F32) * (top * (1.0 / LEVELS))

    def give(total, dest, k, way, i, to):
        q_out[dest, k], s_out[dest, k] = code(total)
        for copy in hop(dest, k, way, i, to):
            copy.start()

    def add_squares(total):
        squares[...] += jnp.sum((total * total).reshape(half // 8, 8, tile), axis=0)

    def place(i, first, second):
        dest = jnp.where(i < units, first, second)
        return dest, jnp.where(i < units, i, lax.rem(i + RES, units))

    def shadowed(k):
        return k // 4 * 2 + k % 2 >= blocks - SHADOW

    def lend(first, last):
        for at in range(first, last):
            n, i = at // 3, at % 3
            t = blocks - SHADOW + n
            here = slice(t % 2 * half, (t % 2 + 1) * half)
            value = (m_in, w_in, v_in)[i][here, head_lanes(t // 2)]
            refs = [shadow_q]
            if i < 2:
                shadow_q[i, n], shadow_s[i, n] = code(value)
                refs.append(shadow_s)
            else:
                root = (jnp.sqrt(value) - ROOT_MID) * (LEVELS / ROOT_SPAN)
                shadow_q[i, n] = jnp.round(root).astype(jnp.int32).astype(jnp.int16)
            for j, ref in enumerate(refs):
                pltpu.make_async_remote_copy(
                    src_ref=ref.at[i, n],
                    dst_ref=ref.at[i, n],
                    send_sem=shadow_sem.at[j],
                    recv_sem=shadow_sem.at[2 + j],
                    device_id={"dp": behind},
                    device_id_type=MESH,
                ).start()

    squares[...] = jnp.zeros(squares.shape, F32)

    def hello(stage):
        slot = stage + 1
        pl.semaphore_signal(
            meet.at[stage], inc=1, device_id={"mp": peer(slot)}, device_id_type=MESH
        )

    def heard(stage):
        pl.semaphore_wait(meet.at[stage], 1)

    def send(i):
        dest, k = place(i, far_end, far_mid)
        dest = jnp.where(i < 2 * units, dest, mid)
        k = jnp.where(i < 2 * units, k, i - 2 * units)
        give(acc[dest, *unit(k)], dest, k, 0, i, ahead)

    @pl.when(at_end)
    def _():
        own_act(far_end).wait()
        own_vg(0).wait()
        for k in range(2):
            for part in range(2):
                multiply_unit(far_end, part, k, 0)
        for k in range(2):
            for part in range(2):
                with jax.named_scope(f"Ew{k}{part}"):
                    if k == 0:
                        pair_act(far_end, part).wait_recv()
                    if part == 0:
                        pair_vg(0, k).wait_recv()
                with jax.named_scope(f"Em{k}{part}"):
                    multiply_unit(far_end, part, k, 1)
                    send(2 * k + part)

        for slot in range(1, heads):
            with jax.named_scope(f"Em{slot}"):
                ready_vg(slot)
                multiply(far_end, slot)
                for k in range(4):
                    send(4 * slot + k)

        for copy in loads:
            copy.start()
        with jax.named_scope("Erest"):
            ready(far_mid)

            @pl.loop(0, heads)
            def _(slot):
                multiply(far_mid, slot)

            @pl.loop(units, 2 * units)
            def _(i):
                send(i)

            ready(mid)

            @pl.loop(0, heads)
            def _(slot):
                multiply(mid, slot)

            @pl.loop(2 * units, 2 * units + RES + EARLY)
            def _(i):
                send(i)

            ready(end)

            @pl.loop(0, heads)
            def _(slot):
                multiply(end, slot)

        @pl.loop(0, 2 * units - RES)
        def _(j):
            with jax.named_scope("Et"):
                dest, k = place(j, end, mid)
                total = take(dest, k, 1, j)
                add_squares(total)

                @pl.when(j < units)
                def _():
                    acc[dest, *unit(k)] = total

                @pl.when((j >= units) & shadowed(k))
                def _():
                    q, top = code(total)
                    q_out[mid, k], s_out[mid, k] = q, top
                    q_in[0, mid, k], s_in[0, mid, k] = q, top

                @pl.when(j == 1)
                def _():
                    hello(0)

                @pl.when(j == units // 2)
                def _():
                    heard(0)
                    hello(1)

        heard(1)

    @pl.when(jnp.logical_not(at_end))
    def _():
        with jax.named_scope("Ml"):
            for copy in loads:
                copy.wait()
            lend(0, LENT[0])
        own_act(far_end).wait()
        own_vg(0).wait()
        for part in range(2):
            pair_act(far_end, part).wait_recv()
            pair_vg(0, part).wait_recv()
        for slot in range(heads):
            with jax.named_scope(f"Mm{slot}"):
                if slot:
                    ready_vg(slot)
                multiply(far_end, slot)
        for dest in order[1:]:
            ready(dest)

        def onward(j):
            dest, k = place(j, end, mid)
            total = take(dest, k, 1, j)

            @pl.when(j < 2 * units - RES)
            def _():
                give(total, dest, k, 1, j, behind)

            @pl.when(j >= units)
            def _():
                acc[dest, *unit(k)] = total

        @pl.loop(0, 2 * units)
        def _(i):
            with jax.named_scope("Mn"):
                dest, k = place(i, far_end, far_mid)
                give(take(dest, k, 0, i), dest, k, 1, i, ahead)

            @pl.when(i < 3 * heads)
            def _():
                dest = jnp.where(i < heads, end, jnp.where(i < 2 * heads, far_mid, mid))
                multiply(dest, lax.rem(i, heads))

            @pl.when(i >= LAG)
            def _():
                with jax.named_scope("Mf"):
                    onward(i - LAG)

            @pl.when(i == LAG + 1)
            def _():
                hello(0)

            @pl.when(i == LAG + units // 2)
            def _():
                heard(0)
                hello(1)

        left = min(LAG, RES)

        @pl.loop(2 * units - LAG, 2 * units - left)
        def _(j):
            with jax.named_scope("Mf"):
                onward(j)

        lend(*LENT)

        @pl.loop(0, RES)
        def _(k):
            with jax.named_scope("Mr"):
                @pl.when(k < left)
                def _():
                    onward(2 * units - left + k)

                total = take(mid, k, 0, 2 * units + k)
                acc[mid, *unit(k)] = total
                add_squares(total)

        heard(1)

    me = dp * heads + mp
    norms[me] = jnp.sum(squares[...], axis=0, keepdims=True)

    def norm_to(at_z, other, slot):
        return pltpu.make_async_remote_copy(
            src_ref=norms.at[me],
            dst_ref=norms.at[me],
            send_sem=norm_sem.at[0],
            recv_sem=norm_sem.at[1],
            device_id={"dp": at_z * 2 + lax.rem(core + other, 2), "mp": peer(slot)},
            device_id_type=MESH,
        )

    def taken(ref, sem):
        pltpu.make_async_copy(ref, ref, sem).wait()

    others = [
        (at_z, other, slot)
        for i, at_z in enumerate((far_end, far_mid, jnp.where(at_end, mid, end), z))
        for slot in range(heads - 1, -1, -1)
        for other in (1, 0)
        if i < 3 or other or slot
    ]
    with jax.named_scope("ns"):
        for at in others:
            norm_to(*at).start()

    @pl.when(at_end)
    def _():
        @pl.loop(2 * units + RES + EARLY, 3 * units)
        def _(i):
            k = i - 2 * units

            @pl.when(shadowed(k))
            def _():
                for copy in hop(mid, k, 0, i, ahead):
                    copy.start()

            @pl.when(jnp.logical_not(shadowed(k)))
            def _():
                send(i)

        for copy in loads:
            copy.wait()

    @pl.when(jnp.logical_not(at_end))
    def _():
        with jax.named_scope("Ml2"):
            lend(LENT[1], 3 * SHADOW)

    with jax.named_scope("nw"):
        taken(norms.at[pl.ds(0, len(others))], norm_sem.at[1])
    square_sum = jnp.sum(jnp.sum(norms[...], axis=0), keepdims=True)
    factor = jnp.minimum(1.0, clip_total / (jnp.sqrt(square_sum) + 1e-06))
    step_count = jnp.full((1, 1), step_ref[0].astype(F32), F32)
    scale_first, scale_second = adam_terms(step_count)

    def block(owner, origin, part):
        start = (owner * dpn + origin) * rows + part * half
        return rollout_ref.at[pl.ds(pl.multiple_of(start, half), half)]

    def piece(head, part):
        return update.at[head * 2 + part]

    def mine(part):
        return pltpu.make_async_copy(
            piece(mp, part), block(mp, dp, part), in_sem.at[line + 3]
        )

    def to_head(slot, part):
        return pltpu.make_async_remote_copy(
            src_ref=piece(peer(slot), part),
            dst_ref=block(mp, dp, part),
            send_sem=a2a_send.at[0],
            recv_sem=near_recv.at[slot * 2 + part],
            device_id={"mp": peer(slot)},
            device_id_type=MESH,
        )

    def to_shadow(at):
        t = blocks - SHADOW + at
        return pltpu.make_async_remote_copy(
            src_ref=update.at[blocks + at],
            dst_ref=block(mp, mid * 2 + core, t % 2),
            send_sem=shadow_sem.at[0],
            recv_sem=near_recv.at[blocks + at],
            device_id={"mp": peer(t // 2)},
            device_id_type=MESH,
        )

    def relay(ref, owner, at_z, part, send, recv, to):
        return pltpu.make_async_remote_copy(
            src_ref=ref,
            dst_ref=block(owner, at_z * 2 + core, part),
            send_sem=send,
            recv_sem=recv,
            device_id={"dp": to},
            device_id_type=MESH,
        )

    def send_ahead(ref, owner, at_z, part, sem=0):
        recv = wide_recv.at[(at_z * heads + owner) * 2 + part]
        return relay(ref, owner, at_z, part, in_sem.at[sem], recv, ahead)

    def send_behind(ref, owner, at_z, part):
        recv = wide_recv.at[(at_z * heads + owner) * 2 + part]
        return relay(ref, owner, at_z, part, in_sem.at[2], recv, behind)

    def send_mate(ref, owner, at_z, part):
        return relay(ref, owner, at_z, part, in_sem.at[3], mate_recv.at[0], mate)

    def spread(ref, owner, part, back=True):
        if back:

            @pl.when(jnp.logical_not(at_end))
            def _():
                send_behind(ref, owner, z, part).start()

        send_ahead(ref, owner, z, part).start()
        send_mate(ref, owner, z, part).start()

    def spread_slab(r):
        here = pl.ds(r * slab, slab)
        start = pl.multiple_of((mp * dpn + dp) * rows + r * slab, slab)
        recv = wide_recv.at[(z * heads + mp) * 2]

        def copy(i, recv, to):
            return pltpu.make_async_remote_copy(
                src_ref=update.at[mp * 2, here],
                dst_ref=rollout_ref.at[pl.ds(start, slab)],
                send_sem=in_sem.at[i],
                recv_sem=recv,
                device_id={"dp": to},
                device_id_type=MESH,
            )

        @pl.when(jnp.logical_not(at_end))
        def _():
            copy(2, recv, behind).start()

        copy(0, recv, ahead).start()
        copy(3, mate_recv.at[0], mate).start()

    def from_ahead(at_z, slot, part):
        owner = source(slot)
        ref = block(owner, at_z * 2 + core, part)
        send_ahead(ref, owner, at_z, part).wait_recv()

        @pl.when(jnp.logical_not(at_end))
        def _():
            send_behind(ref, owner, at_z, part).start()

        send_mate(ref, owner, at_z, part).start()

    def from_behind(slot, part):
        owner = source(slot)
        ref = block(owner, end * 2 + core, part)
        send_ahead(ref, owner, end, part).wait_recv()
        send_ahead(ref, owner, end, part, 1).start()
        send_mate(ref, owner, end, part).start()

    def from_plane(slot, part):
        to_head(slot, part).wait_recv()
        back = slot * 2 + part < blocks - SHADOW
        spread(block(source(slot), dp, part), source(slot), part, back)

    def from_shadow(at):
        t = blocks - SHADOW + at
        owner = source(t // 2)
        to_shadow(at).wait_recv()
        send_mate(block(owner, mid * 2 + core, t % 2), owner, mid, t % 2).start()

    slab = min(32, half)

    def step_rows(slot, part, first=0, last=half // slab):
        lanes = head_lanes(slot)

        @pl.loop(first, last)
        def _(r):
            at = pl.ds(pl.multiple_of(part * half + r * slab, slab), slab)
            clipped = acc[z, at, lanes] * factor
            weight = w_in[at, lanes]
            first = 0.9 * m_in[at, lanes] + 0.1 * clipped
            second = 0.95 * v_in[at, lanes] + 0.05 * clipped * clipped
            m_out[at, lanes] = first
            v_out[at, lanes] = second
            direction = (first * scale_first) / (
                jnp.sqrt(second * scale_second) + 1e-08
            ) + 0.1 * weight
            w_out[at, lanes] = weight - 0.01 * direction
            here = pl.ds(pl.multiple_of(r * slab, slab), slab)
            update[peer(slot) * 2 + part, here, :] = direction.astype(jnp.bfloat16)

    def shadow_rows(at):
        t = blocks - SHADOW + at
        slot, part = t // 2, t % 2
        to = jnp.where(at_end, blocks + at, peer(slot) * 2 + part)

        @pl.loop(0, half // slab)
        def _(r):
            here = pl.ds(pl.multiple_of(r * slab, slab), slab)
            for c in range(2):
                k = 4 * slot + 2 * c + part
                lanes = slice(c * tile, (c + 1) * tile)
                first, weight = (
                    decode(shadow_q[i, at, here, lanes], shadow_s[i, at, :, lanes])
                    for i in range(2)
                )
                root = shadow_q[2, at, here, lanes].astype(jnp.int32).astype(F32)
                root = root * (ROOT_SPAN / LEVELS) + ROOT_MID
                second = root * root
                clipped = decode(q_in[0, mid, k, here, :], s_in[0, mid, k]) * factor
                first = 0.9 * first + 0.1 * clipped
                second = 0.95 * second + 0.05 * clipped * clipped
                direction = (first * scale_first) / (
                    jnp.sqrt(second * scale_second) + 1e-08
                ) + 0.1 * weight
                update[to, here, lanes] = direction.astype(jnp.bfloat16)

    def late(slot):
        @pl.when(jnp.logical_not(at_end))
        def _():
            for k in range(max(4 * slot, RES), 4 * slot + 4):
                if shadowed(k):
                    arrived(0, 2 * units + k)
                    acc[mid, *unit(k)] = decode(q_in[0, mid, k], s_in[0, mid, k])
                else:
                    acc[mid, *unit(k)] = take(mid, k, 0, 2 * units + k)

    work = [(slot, part) for slot in range(heads) for part in range(2)]
    for slot, part in work:
        with jax.named_scope(f"up{slot}{part}"):
            at = slot * 2 + part - (blocks - SHADOW)
            if part == 0 and 4 * slot + 4 > RES:
                late(slot)
            if slot + part == 0:
                for r in range(half // slab):
                    step_rows(0, 0, r, r + 1)
                    spread_slab(r)
            else:
                step_rows(slot, part)
            if at >= 0:

                @pl.when(jnp.logical_not(at_end))
                def _():
                    shadow_rows(at)

            if slot == 0:
                mine(part).start()
                if part:
                    spread(piece(mp, part), mp, part)
            else:
                to_head(slot, part).start()

    stores = [
        pltpu.make_async_copy(src, dst, in_sem.at[line + i])
        for i, (src, dst) in enumerate(
            ((w_out, new_master_ref), (m_out, new_first_ref), (v_out, new_second_ref))
        )
    ]
    for copy in stores:
        copy.start()

    @pl.when(at_end)
    def _():
        with jax.named_scope("Es"):
            for j, ref in enumerate((shadow_q, shadow_s)):
                taken(ref, shadow_sem.at[2 + j])
            for at in range(SHADOW):
                shadow_rows(at)
                to_shadow(at).start()
        with jax.named_scope("Eaa"):
            for slot, part in work[2:]:
                from_plane(slot, part)
            for slot, part in work[: blocks - SHADOW]:
                from_ahead(mid, slot, part)
            for at in range(SHADOW):
                from_shadow(at)
        for at_z in (far_mid, far_end):
            with jax.named_scope("Efar"):
                for slot, part in work:
                    from_ahead(at_z, slot, part)

    @pl.when(jnp.logical_not(at_end))
    def _():
        for t, (slot, part) in enumerate(work[2:]):
            if t < 3:
                with jax.named_scope(f"Mah{t}"):
                    from_ahead(far_mid, *work[t])
            with jax.named_scope(f"Maa{t}"):
                from_plane(slot, part)
        for t in range(8):
            with jax.named_scope(f"Mfar{t}"):
                if t >= 3:
                    from_ahead(far_mid, *work[t])
                from_behind(*work[t])
        with jax.named_scope("Mfare"):
            for slot, part in work:
                from_ahead(far_end, slot, part)

    with jax.named_scope("tail"):
        plane = heads * rows
        taken(rollout_ref.at[pl.ds(0, line * plane)], mate_recv.at[0])
        taken(rollout_ref.at[pl.ds(0, line * plane)], in_sem.at[3])
        taken(rollout_ref.at[pl.ds(0, plane)], in_sem.at[0])

        @pl.when(jnp.logical_not(at_end))
        def _():
            taken(rollout_ref.at[pl.ds(0, plane)], in_sem.at[1])
            back = (line - 1) * plane - SHADOW * half
            taken(rollout_ref.at[pl.ds(0, back)], in_sem.at[2])
            for j, ref in enumerate((shadow_q, shadow_s)):
                taken(ref, shadow_sem.at[j])

        @pl.when(at_end)
        def _():
            taken(update.at[pl.ds(0, SHADOW)], shadow_sem.at[0])

        taken(update.at[pl.ds(0, blocks - 2)], a2a_send.at[0])
        taken(norms.at[pl.ds(0, len(others))], norm_sem.at[0])
        taken(act.at[:, pl.ds(0, tokens)], pair_send.at[0])
        taken(vg.at[pl.ds(0, tokens)], pair_send.at[1])
        for i, ref in enumerate((q_out, s_out)):
            for dest in (far_end, far_mid):
                taken(ref.at[dest], rs_send.at[i, dest])

            @pl.when(at_end)
            def _():
                taken(ref.at[mid], rs_send.at[i, mid])

            @pl.when(jnp.logical_not(at_end))
            def _():
                taken(ref.at[end], rs_send.at[i, end])
                taken(ref.at[mid, pl.ds(RES, units - RES)], rs_send.at[i, mid])

        taken(update.at[pl.ds(0, 2)], in_sem.at[line + 3])
        for copy in stores:
            copy.wait()


def settle(*refs):
    count = (len(refs) - 1) // 2
    sem = refs[-1]
    copies = []
    for i in range(count):
        source, place = refs[i], refs[count + i]
        piece = source.shape[0] // PIECES[i]
        for j in range(PIECES[i]):
            at = pl.ds(j * piece, piece)
            copies.append(
                pltpu.make_async_copy(source.at[at], place.at[at], sem.at[len(copies)])
            )
    for copy in copies:
        copy.start()
    for copy in copies:
        copy.wait()


def one_kernel(line, heads, activations, value_grad, master, first_moment, second_moment, step_count):
    rows, cols = master.shape
    tokens = activations.shape[0]
    tile = cols // heads // 2
    units = 4 * heads
    dpn = 2 * line
    clip_total = 0.5 * math.sqrt(rows * dpn * heads * cols)
    hbm = pl.BlockSpec(memory_space=pl.ANY)
    owned = jax.ShapeDtypeStruct((rows, cols), F32)
    wide = pltpu.VMEM((rows, cols), F32)
    dma = pltpu.SemaphoreType.DMA
    results = pl.pallas_call(
        functools.partial(kernel, line, heads, clip_total),
        out_shape=(
            owned,
            owned,
            owned,
            jax.ShapeDtypeStruct((rows * dpn * heads, cols // heads), jnp.bfloat16),
        ),
        in_specs=[pl.BlockSpec(memory_space=pltpu.SMEM)] + [hbm] * 5,
        out_specs=(hbm,) * 4,
        scratch_shapes=[
            pltpu.VMEM((line, 2 * tokens, rows), jnp.bfloat16),
            pltpu.VMEM((2 * tokens, cols), jnp.bfloat16),
            pltpu.VMEM((line, rows, cols), F32),
            pltpu.VMEM((line, units, rows // 2, tile), jnp.int16),
            pltpu.VMEM((line, units, 1, tile), F32),
            pltpu.VMEM((2, line, units, rows // 2, tile), jnp.int16),
            pltpu.VMEM((2, line, units, 1, tile), F32),
            pltpu.VMEM((8, tile), F32),
            pltpu.VMEM((dpn * heads, 1, tile), F32),
            pltpu.VMEM((rows // 4 + 1, 1, tile), F32),
            wide,
            wide,
            wide,
            wide,
            wide,
            wide,
            pltpu.VMEM((2 * heads + SHADOW, rows // 2, 2 * tile), jnp.bfloat16),
            pltpu.VMEM((3, SHADOW, rows // 2, 2 * tile), jnp.int16),
            pltpu.VMEM((2, SHADOW, 1, 2 * tile), F32),
            dma((line + heads,)),
            dma((2,)),
            dma((line + heads + 2,)),
            dma((3,)),
            dma((2, line)),
            dma((3 * units,)),
            dma((2 * units,)),
            pltpu.SemaphoreType.REGULAR((2,)),
            dma((2,)),
            dma((4,)),
            dma((1,)),
            dma((1,)),
        ],
        compiler_params=pltpu.CompilerParams(
            collective_id=0, has_side_effects=True, vmem_limit_bytes=28 * 1024 * 1024
        ),
    )(
        step_count,
        *(
            pltpu.with_memory_space_constraint(x, pltpu.HBM)
            for x in (activations, value_grad, master, first_moment, second_moment)
        ),
    )
    shapes = tuple(jax.ShapeDtypeStruct(x.shape, x.dtype) for x in results)
    return pl.pallas_call(
        settle,
        out_shape=shapes,
        in_specs=[hbm] * 4,
        out_specs=(hbm,) * 4,
        scratch_shapes=[dma((sum(PIECES),))],
        compiler_params=pltpu.CompilerParams(vmem_limit_bytes=4 * 1024 * 1024),
    )(*(pltpu.with_memory_space_constraint(x, pltpu.VMEM) for x in results))


def plain(activations, value_grad, master, first_moment, second_moment, step_count):
    own_rows, cols = master.shape
    grad = lax.psum_scatter(
        lax.dot_general(
            activations, value_grad, (((0,), (0,)), ((), ())), preferred_element_type=F32
        ),
        "dp",
        scatter_dimension=0,
        tiled=True,
    )
    square_sum = lax.psum(jnp.sum(grad * grad), ("dp", "mp"))
    head_count = lax.axis_size("mp")
    clip_total = 0.5 * math.sqrt(own_rows * lax.axis_size("dp") * head_count * cols)
    factor = jnp.minimum(jnp.float32(1.0), clip_total / (jnp.sqrt(square_sum) + 1e-06))
    clipped = factor * grad
    new_first = 0.9 * first_moment + 0.1 * clipped
    new_second = 0.95 * second_moment + 0.05 * clipped * clipped
    scale_first, scale_second = adam_terms(step_count[0].astype(F32))
    direction = new_first * scale_first / (jnp.sqrt(new_second * scale_second) + 1e-08) + 0.1 * master
    new_master = master - 0.01 * direction
    update = direction.astype(jnp.bfloat16)
    received = lax.all_to_all(update, "mp", split_axis=1, concat_axis=0, tiled=True)
    stacked = received.reshape(head_count, own_rows, received.shape[1])
    gathered = lax.all_gather(stacked, "dp", axis=1, tiled=True)
    return (new_master, new_first, new_second, gathered.reshape(-1, gathered.shape[2]))


def solution(mesh):
    dpn, heads = mesh.shape["dp"], mesh.shape["mp"]

    def on_device(*args):
        rows, cols = args[2].shape
        if dpn == 8 and heads == 4 and rows % 64 == 0 and (cols // heads) % 256 == 0:
            return one_kernel(dpn // 2, heads, *args)
        return plain(*args)

    in_specs = (
        P("dp", "mp"),
        P("dp", None),
        P(("mp", "dp"), None),
        P(("mp", "dp"), None),
        P(("mp", "dp"), None),
        P(),
    )
    out_specs = (P(("mp", "dp"), None), P(("mp", "dp"), None), P(("mp", "dp"), None), P(None, "mp"))
    return jax.shard_map(
        on_device, mesh=mesh, in_specs=in_specs, out_specs=out_specs, check_vma=False
    )
```
